32 devices in a mesh: rec: 2 (over y), gx: 16 (over z, x, core).
Axes of the slice: x: 2, y: 2, z: 4, core: 2. Of those that a mesh axis runs over, the one named last changes fastest.
Arguments:
- velocity: float32 [4, 3, 96, 16, 128], P(None, None, ('rec', 'gx')), parts along dimension 2, may hold values from -6 to 36, as said below
- span_rim: float32 [4, 2, 96, 10, 6], P(None, None, ('rec', 'gx')), parts along dimension 2, may hold values from -6 to 36, as said below
- sketch_old: bfloat16 [3, 96, 10, 128, 256], P(None, ('rec', 'gx')), parts along dimension 1, as said below
- omega: float32 [4, 256], replicated, may hold values from -6 to 6
Outputs:
- basis: bfloat16 [3, 96, 10, 128, 256], P(None, ('rec', 'gx')), parts along dimension 1
- factor: float32 [512, 256], P('rec'), parts along dimension 0
The draws below stay inside these ranges and needn't reach their ends.
There are 2 independent parts, one for each index of `rec`. The reference program is written for one: setup_inputs(seed, part) draws one part's arguments, and reference() takes and returns one part's arrays. A program takes and returns all parts, laid end to end along the dimension named above; an argument that names none is the same for every part. Nothing has to cross between parts.
Inputs may be any that keep to these rules, and one draw needn't show every extreme that they name: `sketch_old`: finite values of order one; rows differ in scale. `velocity`: finite values. `span_rim`: finite values.
All inputs are finite; a program needn't handle non-finite values.
Results may differ from the reference program's by a relative error of at most 0.014.
The reference program's roundings to bfloat16 on the way (of `sketch` and `inverse_one`) count: a program that leaves them out, or rounds other values in their place, can miss the bound.
Values sent between devices are 32-bit elements; how exact they have to be, the bound alone decides.
No kernel may reach another device: no remote copies, remote signals or barrier semaphores. Data moves between devices by JAX's collectives and lax.ppermute only.
A program may use at most 64 MiB of HBM per device.

```python
import jax
import jax.numpy as jnp
from jax import lax

RANK = 256
SNAPS = 4
NY = 10
NZ = 128
NX = 48


def flow_profile(rows, offset, base, spread):
    position = (jnp.arange(rows, dtype=jnp.float32) + offset + 0.5) / (NY + 6)
    return base + spread * jnp.tanh(2.0 * position - 1.0)


def draw_velocity(key, part):
    key_a = jax.random.fold_in(key, 21)
    shape = (SNAPS, 3, NX, NY + 6, NZ)
    values = jnp.clip(jax.random.normal(key_a, shape, jnp.float32), -6.0, 6.0)
    profile = flow_profile(NY + 6, 0, 16.0, 6.0)
    first = (jnp.arange(3, dtype=jnp.int32) == 0).astype(jnp.float32).reshape(1, 3, 1, 1, 1)
    values = values + first * profile.reshape(1, 1, 1, NY + 6, 1)
    return values.astype(jnp.float32)


def draw_span_rim(key, part):
    key_a = jax.random.fold_in(key, 31)
    shape = (SNAPS, 2, NX, NY, 6)
    values = jnp.clip(jax.random.normal(key_a, shape, jnp.float32), -6.0, 6.0)
    profile = flow_profile(NY, 3, 16.0, 6.0)
    first = (jnp.arange(2, dtype=jnp.int32) == 0).astype(jnp.float32).reshape(1, 2, 1, 1, 1)
    values = values + first * profile.reshape(1, 1, 1, NY, 1)
    return values.astype(jnp.float32)


def draw_sketch_old(key, part):
    key_a = jax.random.fold_in(key, 11)
    key_b = jax.random.fold_in(key, 12)
    shape = (3, NX, NY, NZ, RANK)
    position = (jnp.arange(NX, dtype=jnp.float32) + 0.5) / NX
    slab_scale = (0.6 + 1.2 * position).reshape(1, NX, 1, 1, 1)
    rough = jnp.exp(jax.random.uniform(key_b, (3, NX, NY, NZ, 1), jnp.float32, -0.35, 0.35))
    values = jax.random.normal(key_a, shape, jnp.float32)
    values = jnp.clip(values * slab_scale * rough, -8.0, 8.0)
    return values.astype(jnp.bfloat16)


def gaussian(stream_key, extent, width, most, kind=jnp.bfloat16):
    result = width * jax.random.normal(stream_key, extent, jnp.float32)
    return jnp.clip(result, min=-most, max=most).astype(kind)


def setup_inputs(seed: int = 0, part: int = 0) -> dict:
    seeds = jax.random.split(jax.random.key(seed), 5)
    part_splits = jax.random.split(jax.random.fold_in(seeds[4], part), 5)
    return {
        "velocity": draw_velocity(jax.random.fold_in(jax.random.fold_in(seeds[4], part), 71), part),
        "span_rim": draw_span_rim(jax.random.fold_in(jax.random.fold_in(seeds[4], part), 71), part),
        "sketch_old": draw_sketch_old(jax.random.fold_in(jax.random.fold_in(seeds[4], part), 71), part),
        "omega": gaussian(seeds[3], (SNAPS, RANK), 1.0, 6.0, jnp.float32),
    }


COEFS = (0.75, -0.15, 1.0 / 60.0)

def periodic_diff(field, axis):
    total = jnp.zeros(field.shape, jnp.float32)
    for shift_k, weight in zip((1, 2, 3), COEFS):
        total = total + weight * (jnp.roll(field, -shift_k, axis) - jnp.roll(field, shift_k, axis))
    return total

def band_diff(padded, axis, count):
    out_shape = list(padded.shape)
    out_shape[axis] = count
    total = jnp.zeros(tuple(out_shape), jnp.float32)
    for shift_k, weight in zip((1, 2, 3), COEFS):
        ahead = lax.slice_in_dim(padded, 3 + shift_k, 3 + shift_k + count, axis=axis)
        behind = lax.slice_in_dim(padded, 3 - shift_k, 3 - shift_k + count, axis=axis)
        total = total + weight * (ahead - behind)
    return total

def span_extend(field, rim_part):
    return jnp.concatenate([rim_part[..., :3], field, rim_part[..., 3:]], axis=-1)

def upper_factor(gram):
    order = gram.shape[0]
    index = jnp.arange(order, dtype=jnp.int32)

    def column_step(j, lower):
        pick = (index == j).astype(gram.dtype)
        row = jnp.dot(pick, lower, precision=lax.Precision.HIGHEST)
        column = jnp.dot(gram, pick, precision=lax.Precision.HIGHEST) - jnp.dot(lower, row, precision=lax.Precision.HIGHEST)
        pivot = jnp.sqrt(jnp.sum(column * pick))
        below = (index > j).astype(gram.dtype)
        fresh = column * below / pivot + pick * pivot
        return lower + fresh[:, None] * pick[None, :]
    lower = lax.fori_loop(0, order, column_step, jnp.zeros_like(gram))
    return lower.T

def inverse_upper(upper):
    order = upper.shape[0]
    index = jnp.arange(order, dtype=jnp.int32)
    lower = upper.T

    def row_step(j, solved):
        pick = (index == j).astype(upper.dtype)
        row = jnp.dot(pick, lower, precision=lax.Precision.HIGHEST)
        pivot = jnp.sum(row * pick)
        fresh = (pick - jnp.dot(row, solved, precision=lax.Precision.HIGHEST)) / pivot
        return solved + pick[:, None] * fresh[None, :]
    solved = lax.fori_loop(0, order, row_step, jnp.zeros_like(upper))
    return solved.T

def gram_of(matrix):
    return lax.dot_general(matrix, matrix, (((0,), (0,)), ((), ())), preferred_element_type=jnp.float32)

def reference(velocity, span_rim, sketch_old, omega):
    band = velocity[:, :, :, 3:3 + NY]
    u_span = span_extend(band[:, 0], span_rim[:, 0])
    v_span = span_extend(band[:, 1], span_rim[:, 1])
    vort_x = band_diff(velocity[:, 2], 2, NY) - band_diff(v_span, 3, NZ)
    vort_y = band_diff(u_span, 3, NZ) - periodic_diff(band[:, 2], 1)
    vort_z = periodic_diff(band[:, 1], 1) - band_diff(velocity[:, 0], 2, NY)
    vort = jnp.stack([vort_x, vort_y, vort_z], axis=1)
    sketch = sketch_old.astype(jnp.float32)
    for snap in range(SNAPS):
        sketch = sketch + vort[snap][..., None] * omega[snap]
    sketch = sketch.astype(jnp.bfloat16)
    matrix = sketch.reshape(-1, RANK)
    total = jnp.float32(matrix.shape[0])
    factor = upper_factor(gram_of(matrix) / total)
    inverse_one = inverse_upper(factor).astype(jnp.bfloat16)
    basis = jnp.dot(matrix, inverse_one, preferred_element_type=jnp.float32).astype(jnp.bfloat16)
    return (basis.reshape(sketch.shape), factor)
```

```python
import functools

import jax
import jax.numpy as jnp
from jax import lax
from jax.experimental import pallas as pl
from jax.experimental.pallas import tpu as pltpu
from jax.sharding import PartitionSpec as P

COEFS = (0.75, -0.15, 1.0 / 60.0)


def extended_2(cells, sides, width):
    for axis, dim in sides:
        count = lax.axis_size(axis)
        head = lax.slice_in_dim(cells, 0, width, axis=dim)
        tail = lax.slice_in_dim(cells, cells.shape[dim] - width, cells.shape[dim], axis=dim)
        cells = jnp.concatenate(
            [
                lax.ppermute(tail, axis, [(i, (i + 1) % count) for i in range(count)]),
                cells,
                lax.ppermute(head, axis, [((i + 1) % count, i) for i in range(count)]),
            ],
            axis=dim,
        )
    return cells


def band_diff(padded, axis, count):
    out_shape = list(padded.shape)
    out_shape[axis] = count
    total = jnp.zeros(tuple(out_shape), jnp.float32)
    for shift_k, weight in zip((1, 2, 3), COEFS):
        ahead = lax.slice_in_dim(padded, 3 + shift_k, 3 + shift_k + count, axis=axis)
        behind = lax.slice_in_dim(padded, 3 - shift_k, 3 - shift_k + count, axis=axis)
        total = total + weight * (ahead - behind)
    return total


def span_extend(field, rim_part):
    return jnp.concatenate([rim_part[..., :3], field, rim_part[..., 3:]], axis=-1)


def factor_invert(t_ref, u_ref, x_ref):
    order = t_ref.shape[0]
    lane = lax.broadcasted_iota(jnp.int32, (8, 128), 1)
    sub = lax.broadcasted_iota(jnp.int32, (8, 128), 0)
    full = (8, 128)
    zero = jnp.zeros(full, jnp.float32)
    for p in range(order // 8):
        j0 = 8 * p
        hd = j0 // 128
        c0 = j0 % 128
        halves = [t_ref[j0:j0 + 8, 128 * h:128 * h + 128] for h in range(2)]
        diag = halves[hd]
        in_panel = (lane >= c0) & (lane < c0 + 8)
        ident = jnp.where(lane == sub + c0, 1.0, 0.0)
        halves[hd] = jnp.where(in_panel, ident, diag)
        a = {}
        for j in range(8):
            for i in range(j + 1):
                a[i, j] = jnp.broadcast_to(diag[i:i + 1, c0 + j:c0 + j + 1], full)
        rows = [[jnp.broadcast_to(x[i:i + 1], full) for x in (halves[0], halves[1], diag)] for i in range(8)]
        l = {}
        r = [None] * 8
        rs = [None] * 8
        for k in range(8):
            r[k] = 1.0 / a[k, k]
            rs[k] = lax.rsqrt(a[k, k])
            for i in range(k + 1, 8):
                l[i, k] = a[k, i] * r[k]
            for i in range(k + 1, 8):
                for j in range(i, 8):
                    a[i, j] = a[i, j] - l[i, k] * a[k, j]
                rows[i] = [x - l[i, k] * y for x, y in zip(rows[i], rows[k])]
        z = [None] * 8
        for k in reversed(range(8)):
            zk = [rows[k][h] * r[k] for h in range(2)]
            for i in range(k + 1, 8):
                zk = [x - l[i, k] * y for x, y in zip(zk, z[i])]
            z[k] = zk
        for q in range(p + 1, order // 8):
            rr = slice(8 * q, 8 * q + 8)
            old = [t_ref[rr, 128 * h:128 * h + 128] for h in range(2)]
            m = [jnp.broadcast_to(old[hd][:, c0 + k:c0 + k + 1], full) for k in range(8)]
            acc = [old[0], old[1]]
            acc[hd] = jnp.where(in_panel, 0.0, acc[hd])
            for h in range(2):
                s = m[0] * z[0][h]
                for k in range(1, 8):
                    s = s + m[k] * z[k][h]
                t_ref[rr, 128 * h:128 * h + 128] = acc[h] - s
        outs = [zero, zero, zero]
        for k in range(8):
            outs = [jnp.where(sub == k, rows[k][c] * rs[k], outs[c]) for c in range(3)]
        for h in range(2):
            col = lane + 128 * h
            src = outs[2] if h == hd else outs[h]
            u_ref[j0:j0 + 8, 128 * h:128 * h + 128] = jnp.where(col >= sub + j0, src, 0.0)
            x_ref[j0:j0 + 8, 128 * h:128 * h + 128] = jnp.where(col <= sub + j0, outs[h], 0.0)


def pack_kernel(parity_ref, gram_ref, keep_ref, send_ref):
    half = gram_ref.shape[0] // 2
    row = lax.broadcasted_iota(jnp.int32, (half, half), 0)
    col = lax.broadcasted_iota(jnp.int32, (half, half), 1)
    low = gram_ref[half:, half:]
    mixed = jnp.where(row <= col, gram_ref[:half, :half], low)
    diag = jnp.sum(jnp.where(row == col, low, 0.0), axis=0, keepdims=True)
    packed = jnp.concatenate([gram_ref[:half, half:], mixed], axis=1)
    part = half // 2
    extra = jnp.broadcast_to(jnp.concatenate([diag, diag], axis=1), (8, 2 * half))
    first = parity_ref[0] == 0
    upper, lower = packed[:part], packed[part:]
    keep_ref[:part] = jnp.where(first, upper, lower)
    send_ref[:part] = jnp.where(first, lower, upper)
    keep_ref[part:] = extra
    send_ref[part:] = extra


def factor_kernel(scale, parity_ref, mine_ref, other_ref, upper_ref, inverse_ref, work_ref, solved_ref):
    order = work_ref.shape[0]
    half = order // 2
    part = half // 2
    first = parity_ref[0] == 0
    mine, other = mine_ref[...] * scale, other_ref[...] * scale
    packed = jnp.concatenate([jnp.where(first, mine[:part], other[:part]), jnp.where(first, other[:part], mine[:part])], axis=0)
    cross, mixed = packed[:, :half], packed[:, half:]
    row = lax.broadcasted_iota(jnp.int32, (half, half), 0)
    col = lax.broadcasted_iota(jnp.int32, (half, half), 1)
    turned = mixed.T
    diag = jnp.broadcast_to(mine[part : part + 1, :half], (half, half))
    work_ref[:half, :half] = jnp.where(row <= col, mixed, turned)
    work_ref[:half, half:] = cross
    work_ref[half:, :half] = cross.T
    work_ref[half:, half:] = jnp.where(row > col, mixed, jnp.where(row < col, turned, diag))
    factor_invert(work_ref, upper_ref, solved_ref)
    inverse_ref[...] = solved_ref[...].T.astype(jnp.bfloat16)


def summed_factor(gram, rows, axis):
    count = lax.axis_size(axis)
    order = gram.shape[0]
    parity = (lax.axis_index(axis) % 2).reshape(1)
    in_smem = pl.BlockSpec(memory_space=pltpu.SMEM)
    in_vmem = pl.BlockSpec(memory_space=pltpu.VMEM)
    piece = jax.ShapeDtypeStruct((order // 4 + 8, order), jnp.float32)
    keep, send = pl.pallas_call(
        pack_kernel, out_shape=[piece, piece], in_specs=[in_smem, in_vmem], out_specs=[in_vmem, in_vmem]
    )(parity, gram)
    swap = lambda k: [(i, i ^ k) for i in range(count)]
    total = keep + lax.ppermute(send, axis, swap(1))
    step = 2
    while step < count:
        total = total + lax.ppermute(total, axis, swap(step))
        step *= 2
    other = lax.ppermute(total, axis, swap(1))
    return pl.pallas_call(
        functools.partial(factor_kernel, 1.0 / rows),
        out_shape=[jax.ShapeDtypeStruct((order, order), jnp.float32), jax.ShapeDtypeStruct((order, order), jnp.bfloat16)],
        in_specs=[in_smem, in_vmem, in_vmem],
        out_specs=[in_vmem, in_vmem],
        scratch_shapes=[pltpu.VMEM((order, order), jnp.float32), pltpu.VMEM((order, order), jnp.float32)],
    )(parity, total, other)


def gram_of(matrix):
    return lax.dot_general(
        matrix, matrix, (((0,), (0,)), ((), ())), preferred_element_type=jnp.float32
    )


def local(velocity, span_rim, sketch_old, omega):
    slabs = velocity.shape[2]
    band_rows = velocity.shape[3] - 6
    span_cells = velocity.shape[4]
    extended = extended_2(velocity, (("gx", 2),), 3)
    v_ext = extended[:, 1, :, 3 : 3 + band_rows]
    w_ext = extended[:, 2, :, 3 : 3 + band_rows]
    band = velocity[:, :, :, 3 : 3 + band_rows]
    u_span = span_extend(band[:, 0], span_rim[:, 0])
    v_span = span_extend(band[:, 1], span_rim[:, 1])
    vort_x = band_diff(velocity[:, 2], 2, band_rows) - band_diff(v_span, 3, span_cells)
    vort_y = band_diff(u_span, 3, span_cells) - band_diff(w_ext, 1, slabs)
    vort_z = band_diff(v_ext, 1, slabs) - band_diff(velocity[:, 0], 2, band_rows)
    vort = jnp.stack([vort_x, vort_y, vort_z], axis=1)
    sketch = sketch_old.astype(jnp.float32)
    for snap in range(vort.shape[0]):
        sketch = sketch + vort[snap][..., None] * omega[snap]
    sketch = sketch.astype(jnp.bfloat16)
    matrix = sketch.reshape(-1, sketch.shape[-1])
    rows = matrix.shape[0] * lax.axis_size("gx")
    factor, inverse_one = summed_factor(gram_of(matrix), rows, "gx")
    basis = jnp.dot(matrix, inverse_one, preferred_element_type=jnp.float32).astype(jnp.bfloat16)
    return (basis.reshape(sketch.shape), factor)


def solution(mesh):
    in_specs = (
        P(None, None, ("rec", "gx"), None, None),
        P(None, None, ("rec", "gx"), None, None),
        P(None, ("rec", "gx"), None, None, None),
        P(),
    )
    out_specs = (P(None, ("rec", "gx"), None, None, None), P("rec", None))
    return jax.shard_map(local, mesh=mesh, in_specs=in_specs, out_specs=out_specs, check_vma=False)
```

```python
import functools

import jax
import jax.numpy as jnp
from jax import lax
from jax.experimental import pallas as pl
from jax.experimental.pallas import tpu as pltpu
from jax.sharding import PartitionSpec as P

COEFS = (0.75, -0.15, 1.0 / 60.0)
IN_SMEM = pl.BlockSpec(memory_space=pltpu.SMEM)
IN_VMEM = pl.BlockSpec(memory_space=pltpu.VMEM)
ANYWHERE = pl.BlockSpec(memory_space=pl.ANY)


def wall_diff(plane, count):
    total = jnp.zeros((count, plane.shape[1]), jnp.float32)
    for k, weight in zip((1, 2, 3), COEFS):
        total = total + weight * (plane[3 + k : 3 + k + count] - plane[3 - k : 3 - k + count])
    return total


def span_diff(band, edge):
    cells = band.shape[1]
    lane = lax.broadcasted_iota(jnp.int32, band.shape, 1)
    total = jnp.zeros(band.shape, jnp.float32)
    for k, weight in zip((1, 2, 3), COEFS):
        ahead = pltpu.roll(jnp.where(lane < k, edge, band), cells - k, 1)
        behind = pltpu.roll(jnp.where(lane >= cells - k, edge, band), k, 1)
        total = total + weight * (ahead - behind)
    return total


def stream_diff(planes, at):
    total = jnp.zeros(planes[0].shape, jnp.float32)
    for k, weight in zip((1, 2, 3), COEFS):
        total = total + weight * (planes[at + k] - planes[at - k])
    return total


def parts_of(x):
    high = x.astype(jnp.bfloat16).astype(jnp.float32)
    rest = x - high
    mid = rest.astype(jnp.bfloat16).astype(jnp.float32)
    return high, mid, rest - mid


def update_block(vort, omega, new_ref, acc_ref):
    snaps = len(vort)
    pad = [jnp.zeros((8 - snaps % 8, omega.shape[1]), jnp.float32)] if snaps % 8 else []
    o1, o2, o3 = parts_of(omega)
    right = jnp.concatenate([o1, o2, o1, o3, o1, o2], axis=0).astype(jnp.bfloat16)
    split = [parts_of(v) for v in vort]
    for y in range(vort[0].shape[0]):
        a, b, c = ([s[t][y : y + 1] for s in split] for t in range(3))
        left = jnp.concatenate(a + a + b + a + c + b, axis=0)
        turned = left.T.astype(jnp.bfloat16)
        gain = jnp.dot(turned, right, preferred_element_type=jnp.float32)
        new_ref[y] = (new_ref[y].astype(jnp.float32) + gain).astype(jnp.bfloat16)
    rows, cells, rank = new_ref.shape
    block = new_ref[...].reshape(rows * cells, rank)
    acc_ref[...] += lax.dot_general(block, block, (((0,), (0,)), ((), ())), preferred_element_type=jnp.float32)


def fetch(old_ref, first, new_refs, sems):
    return [
        [
            pltpu.make_async_copy(old_ref.at[first + c, i], new_ref.at[i], sems.at[c, i])
            for i in range(new_ref.shape[0])
        ]
        for c, new_ref in enumerate(new_refs)
    ]


def first_component_kernel(vel_ref, edge_ref, omega_ref, old_ref, new_ref, gram_ref, sems):
    snaps, _, slabs, height, _ = vel_ref.shape
    rows = height - 6
    copies = fetch(old_ref, 0, [new_ref], sems)[0]
    for copy in copies:
        copy.start()
    gram_ref[...] = jnp.zeros_like(gram_ref)
    for i in range(slabs):
        vort = [
            wall_diff(vel_ref[s, 2, i], rows) - span_diff(vel_ref[s, 1, i, 3 : 3 + rows], edge_ref[s, 1, i])
            for s in range(snaps)
        ]
        copies[i].wait()
        update_block(vort, omega_ref[...], new_ref.at[i], gram_ref)


def pack(gram_ref, first, keep_ref, send_ref):
    half = gram_ref.shape[0] // 2
    row = lax.broadcasted_iota(jnp.int32, (half, half), 0)
    col = lax.broadcasted_iota(jnp.int32, (half, half), 1)
    low = gram_ref[half:, half:]
    mixed = jnp.where(row <= col, gram_ref[:half, :half], low)
    diag = jnp.sum(jnp.where(row == col, low, 0.0), axis=0, keepdims=True)
    packed = jnp.concatenate([gram_ref[:half, half:], mixed], axis=1)
    part = half // 2
    extra = jnp.broadcast_to(jnp.concatenate([diag, diag], axis=1), (8, 2 * half))
    upper, lower = packed[:part], packed[part:]
    keep_ref[:part] = jnp.where(first, upper, lower)
    send_ref[:part] = jnp.where(first, lower, upper)
    keep_ref[part:] = extra
    send_ref[part:] = extra


def other_components_kernel(
    parity_ref, vel_ref, edge_ref, behind_ref, ahead_ref, omega_ref, start_ref, old_ref,
    new_y_ref, new_z_ref, keep_ref, send_ref, wide_ref, gram_ref, sems,
):
    snaps, _, slabs, height, _ = vel_ref.shape
    rows = height - 6
    new_refs = [new_y_ref, new_z_ref]
    copies = fetch(old_ref, 1, new_refs, sems)
    for i in range(slabs):
        for c in range(2):
            copies[c][i].start()
    gram_ref[...] = start_ref[...]
    for s in range(snaps):
        for c in range(2):
            for k in range(3):
                at = ((s * 2 + c) * 3 + k) * rows
                wide_ref[s, c, k] = behind_ref[at : at + rows]
                wide_ref[s, c, 3 + slabs + k] = ahead_ref[at : at + rows]
            for i in range(slabs):
                wide_ref[s, c, 3 + i] = vel_ref[s, 1 + c, i, 3 : 3 + rows]
    for i in range(slabs):
        for c in range(2):
            vort = []
            for s in range(snaps):
                along = stream_diff([wide_ref[s, 1 - c, i + k] for k in range(7)], 3)
                if c == 0:
                    vort.append(span_diff(vel_ref[s, 0, i, 3 : 3 + rows], edge_ref[s, 0, i]) - along)
                else:
                    vort.append(along - wall_diff(vel_ref[s, 0, i], rows))
            copies[c][i].wait()
            update_block(vort, omega_ref[...], new_refs[c].at[i], gram_ref)
    pack(gram_ref, parity_ref[0] == 0, keep_ref, send_ref)


def factor_invert(t_ref, u_ref, x_ref):
    order = t_ref.shape[0]
    lane = lax.broadcasted_iota(jnp.int32, (8, 128), 1)
    sub = lax.broadcasted_iota(jnp.int32, (8, 128), 0)
    full = (8, 128)
    zero = jnp.zeros(full, jnp.float32)
    for p in range(order // 8):
        j0 = 8 * p
        hd = j0 // 128
        c0 = j0 % 128
        halves = [t_ref[j0:j0 + 8, 128 * h:128 * h + 128] for h in range(2)]
        diag = halves[hd]
        in_panel = (lane >= c0) & (lane < c0 + 8)
        ident = jnp.where(lane == sub + c0, 1.0, 0.0)
        halves[hd] = jnp.where(in_panel, ident, diag)
        a = {}
        for j in range(8):
            for i in range(j + 1):
                a[i, j] = jnp.broadcast_to(diag[i:i + 1, c0 + j:c0 + j + 1], full)
        rows = [[jnp.broadcast_to(x[i:i + 1], full) for x in (halves[0], halves[1], diag)] for i in range(8)]
        l = {}
        r = [None] * 8
        rs = [None] * 8
        for k in range(8):
            r[k] = 1.0 / a[k, k]
            rs[k] = lax.rsqrt(a[k, k])
            for i in range(k + 1, 8):
                l[i, k] = a[k, i] * r[k]
            for i in range(k + 1, 8):
                for j in range(i, 8):
                    a[i, j] = a[i, j] - l[i, k] * a[k, j]
                rows[i] = [x - l[i, k] * y for x, y in zip(rows[i], rows[k])]
        z = [None] * 8
        for k in reversed(range(8)):
            zk = [rows[k][h] * r[k] for h in range(2)]
            for i in range(k + 1, 8):
                zk = [x - l[i, k] * y for x, y in zip(zk, z[i])]
            z[k] = zk
        for q in range(p + 1, order // 8):
            rr = slice(8 * q, 8 * q + 8)
            old = [t_ref[rr, 128 * h:128 * h + 128] for h in range(2)]
            m = [jnp.broadcast_to(old[hd][:, c0 + k:c0 + k + 1], full) for k in range(8)]
            acc = [old[0], old[1]]
            acc[hd] = jnp.where(in_panel, 0.0, acc[hd])
            for h in range(2):
                s = m[0] * z[0][h]
                for k in range(1, 8):
                    s = s + m[k] * z[k][h]
                t_ref[rr, 128 * h:128 * h + 128] = acc[h] - s
        outs = [zero, zero, zero]
        for k in range(8):
            outs = [jnp.where(sub == k, rows[k][c] * rs[k], outs[c]) for c in range(3)]
        for h in range(2):
            col = lane + 128 * h
            src = outs[2] if h == hd else outs[h]
            u_ref[j0:j0 + 8, 128 * h:128 * h + 128] = jnp.where(col >= sub + j0, src, 0.0)
            x_ref[j0:j0 + 8, 128 * h:128 * h + 128] = jnp.where(col <= sub + j0, outs[h], 0.0)


def unpack(packed, part_diag, work_ref):
    half = packed.shape[0]
    cross, mixed = packed[:, :half], packed[:, half:]
    row = lax.broadcasted_iota(jnp.int32, (half, half), 0)
    col = lax.broadcasted_iota(jnp.int32, (half, half), 1)
    turned = mixed.T
    diag = jnp.broadcast_to(part_diag[:, :half], (half, half))
    work_ref[:half, :half] = jnp.where(row <= col, mixed, turned)
    work_ref[:half, half:] = cross
    work_ref[half:, :half] = cross.T
    work_ref[half:, half:] = jnp.where(row > col, mixed, jnp.where(row < col, turned, diag))


def basis_kernel(
    scale, parity_ref, mine_ref, other_ref, x_ref, y_ref, z_ref, upper_ref, basis_ref,
    work_ref, solved_ref, stage_ref, sems,
):
    order = work_ref.shape[0]
    part = order // 4
    first = parity_ref[0] == 0
    mine, other = mine_ref[...] * scale, other_ref[...] * scale
    top, bottom = jnp.where(first, mine[:part], other[:part]), jnp.where(first, other[:part], mine[:part])
    unpack(jnp.concatenate([top, bottom], axis=0), mine[part : part + 1], work_ref)
    factor_invert(work_ref, upper_ref, solved_ref)
    inverse = solved_ref[...].T.astype(jnp.bfloat16)
    copies = []
    for c, sketch_ref in enumerate((x_ref, y_ref, z_ref)):
        slabs, rows, cells, rank = sketch_ref.shape
        for i in range(slabs):
            block = sketch_ref[i].reshape(rows * cells, rank)
            product = jnp.dot(block, inverse, preferred_element_type=jnp.float32)
            stage_ref[c, i] = product.astype(jnp.bfloat16).reshape(rows, cells, rank)
            copy = pltpu.make_async_copy(stage_ref.at[c, i], basis_ref.at[c, i], sems.at[c, i])
            copy.start()
            copies.append(copy)
    for copy in copies:
        copy.wait()


def local(velocity, span_rim, sketch_old, omega):
    snaps, _, slabs, height, cells = velocity.shape
    rows = height - 6
    rank = omega.shape[1]
    count = lax.axis_size("gx")
    limit = pltpu.CompilerParams(vmem_limit_bytes=24 << 20)
    place = lax.axis_index("gx")
    parity = (place % 2).reshape(1)
    band = velocity[:, 1:3, :, 3 : 3 + rows]
    tail = band[:, :, slabs - 3 :].reshape(-1, cells)
    head = band[:, :, :3].reshape(-1, cells)
    behind = lax.ppermute(tail, "gx", [(i, (i + 1) % count) for i in range(count)])
    ahead = lax.ppermute(head, "gx", [((i + 1) % count, i) for i in range(count)])
    gap = jnp.zeros((*span_rim.shape[:-1], cells - 6), jnp.float32)
    edge = jnp.concatenate([span_rim[..., 3:], gap, span_rim[..., :3]], axis=-1)
    block = (slabs, rows, cells, rank)
    sketch_x, gram = pl.pallas_call(
        first_component_kernel,
        out_shape=[pltpu.VMEM(block, jnp.bfloat16), jax.ShapeDtypeStruct((rank, rank), jnp.float32)],
        in_specs=[IN_VMEM, IN_VMEM, IN_VMEM, ANYWHERE],
        out_specs=[IN_VMEM, IN_VMEM],
        scratch_shapes=[pltpu.SemaphoreType.DMA((1, slabs))],
        compiler_params=limit,
    )(velocity, edge, omega, sketch_old)
    piece = jax.ShapeDtypeStruct((rank // 4 + 8, rank), jnp.float32)
    sketch_y, sketch_z, keep, send = pl.pallas_call(
        other_components_kernel,
        out_shape=[pltpu.VMEM(block, jnp.bfloat16), pltpu.VMEM(block, jnp.bfloat16), piece, piece],
        in_specs=[IN_SMEM] + [IN_VMEM] * 6 + [ANYWHERE],
        out_specs=[IN_VMEM] * 4,
        scratch_shapes=[
            pltpu.VMEM((snaps, 2, slabs + 6, rows, cells), jnp.float32),
            pltpu.VMEM((rank, rank), jnp.float32),
            pltpu.SemaphoreType.DMA((2, slabs)),
        ],
        compiler_params=limit,
    )(parity, velocity, edge, behind, ahead, omega, gram, sketch_old)
    swap = lambda k: [(i, i ^ k) for i in range(count)]
    total = keep + lax.ppermute(send, "gx", swap(1))
    step = 2
    while step < count:
        total = total + lax.ppermute(total, "gx", swap(step))
        step *= 2
    other = lax.ppermute(total, "gx", swap(1))
    entries = 3 * slabs * rows * cells * count
    factor, basis = pl.pallas_call(
        functools.partial(basis_kernel, 1.0 / entries),
        out_shape=[
            jax.ShapeDtypeStruct((rank, rank), jnp.float32),
            jax.ShapeDtypeStruct((3, *block), jnp.bfloat16),
        ],
        in_specs=[IN_SMEM] + [IN_VMEM] * 5,
        out_specs=[IN_VMEM, ANYWHERE],
        scratch_shapes=[
            pltpu.VMEM((rank, rank), jnp.float32),
            pltpu.VMEM((rank, rank), jnp.float32),
            pltpu.VMEM((3, *block), jnp.bfloat16),
            pltpu.SemaphoreType.DMA((3, slabs)),
        ],
        compiler_params=limit,
    )(parity, total, other, sketch_x, sketch_y, sketch_z)
    return basis, factor


def solution(mesh):
    in_specs = (
        P(None, None, ("rec", "gx"), None, None),
        P(None, None, ("rec", "gx"), None, None),
        P(None, ("rec", "gx"), None, None, None),
        P(),
    )
    out_specs = (P(None, ("rec", "gx"), None, None, None), P("rec", None))
    return jax.shard_map(local, mesh=mesh, in_specs=in_specs, out_specs=out_specs, check_vma=False)
```

```python
import functools

import jax
import jax.numpy as jnp
from jax import lax
from jax.experimental import pallas as pl
from jax.experimental.pallas import tpu as pltpu
from jax.sharding import PartitionSpec as P

COEFS = (0.75, -0.15, 1.0 / 60.0)
IN_SMEM = pl.BlockSpec(memory_space=pltpu.SMEM)
IN_VMEM = pl.BlockSpec(memory_space=pltpu.VMEM)
IN_HBM = pl.BlockSpec(memory_space=pltpu.HBM)
WIDE = 64


def parts_of(x):
    high = x.astype(jnp.bfloat16).astype(jnp.float32)
    rest = x - high
    mid = rest.astype(jnp.bfloat16).astype(jnp.float32)
    return high, mid, rest - mid


def eliminate_below(t_ref, upper, solved, stop):
    order = t_ref.shape[0]
    col = lax.broadcasted_iota(jnp.int32, upper.shape, 1)
    v, w, y = parts_of(jnp.where(col < stop, solved, upper))
    right = jnp.concatenate([v, w, v, y, v, w], axis=0).astype(jnp.bfloat16)
    for base in range(stop // 128 * 128, order, 128):
        a, b, c = parts_of(upper[:, base : base + 128])
        left = jnp.concatenate([a, a, b, a, c, b], axis=0).astype(jnp.bfloat16)
        product = lax.dot_general(left, right, (((0,), (0,)), ((), ())), preferred_element_type=jnp.float32)
        for top in range(max(base, stop), base + 128, WIDE):
            kept = jnp.where((col >= stop - WIDE) & (col < stop), 0.0, t_ref[top : top + WIDE])
            t_ref[top : top + WIDE] = kept - product[top - base : top - base + WIDE]


def factor_block(w_ref, off):
    full = (8, 128)
    sub = lax.broadcasted_iota(jnp.int32, full, 0)
    for j0 in range(0, WIDE, 8):
        c0 = off + j0
        now = w_ref[j0 : j0 + 8]
        rows = [w_ref[pl.ds(j0 + i, 8, stride=0), :] for i in range(8)]
        a = {}
        for j in range(8):
            for i in range(j + 1):
                a[i, j] = jnp.broadcast_to(rows[i][:, c0 + j : c0 + j + 1], full)
        left, scaled, final = {}, {}, {}
        for k in range(0, 8, 2):
            n = k + 1
            top, mid, low = a[k, k], a[k, n], a[n, n]
            rdet = 1.0 / (top * low - mid * mid)
            for i in range(k + 2, 8):
                left[k, i] = (low * a[k, i] - mid * a[n, i]) * rdet
                left[n, i] = (top * a[n, i] - mid * a[k, i]) * rdet
            for i in range(k + 2, 8):
                for j in range(i, 8):
                    a[i, j] = a[i, j] - left[k, i] * a[k, j] - left[n, i] * a[n, j]
                rows[i] = rows[i] - left[k, i] * rows[k] - left[n, i] * rows[n]
            scaled[k] = (low * rows[k] - mid * rows[n]) * rdet
            scaled[n] = (top * rows[n] - mid * rows[k]) * rdet
            root = lax.rsqrt(top)
            ratio = mid * root * root
            final[k] = rows[k] * root
            final[n] = (rows[n] - ratio * rows[k]) * lax.rsqrt(low - mid * ratio)
        for k in reversed(range(8)):
            for i in reversed(range(k // 2 * 2 + 2, 8)):
                scaled[k] = scaled[k] - left[k, i] * scaled[i]
        for q in range(j0 + 8, WIDE, 8):
            old = w_ref[q : q + 8]
            rest = old
            for k in reversed(range(8)):
                rest = rest - jnp.broadcast_to(old[:, c0 + k : c0 + k + 1], full) * scaled[k]
            w_ref[q : q + 8] = rest
        out = final[0]
        for k in range(1, 8):
            out = jnp.where(sub == k, final[k], out)
        w_ref[j0 : j0 + 8] = out


def factor_invert(t_ref, u_ref, x_ref, w_ref):
    order = t_ref.shape[0]
    lane = lax.broadcasted_iota(jnp.int32, (WIDE, 128), 1)
    sub = lax.broadcasted_iota(jnp.int32, (WIDE, 128), 0)
    for b0 in range(0, order, WIDE):
        stop = b0 + WIDE
        half, off = b0 // 128, b0 % 128
        inside = (lane >= off) & (lane < off + WIDE)
        here = slice(128 * half, 128 * half + 128)
        w_ref[...] = jnp.where(inside, t_ref[b0:stop, here], jnp.where(lane == sub + (WIDE - off), 1.0, 0.0))
        factor_block(w_ref, off)
        done = w_ref[...]
        moved = pltpu.roll(done, 64, 1)
        low, high = (moved, done) if off == 0 else (done, moved)
        x1, x2, x3 = parts_of(low)
        y1, y2, _ = parts_of(high)
        r1, r2, r3 = parts_of(t_ref[b0:stop])
        pair = lambda p, q: jnp.where(lane < WIDE, p, q)
        first = jnp.concatenate([pair(x1, y1), pair(x2, y1), pair(x3, y2)], axis=1).astype(jnp.bfloat16)
        second = jnp.concatenate([r1, r2, r1, r3, r1, r2], axis=0).astype(jnp.bfloat16)
        rows = jnp.dot(first, second, preferred_element_type=jnp.float32)
        upper, solved = [], []
        for h in range(order // 128):
            wide = rows[:, 128 * h : 128 * h + 128]
            zero = jnp.zeros_like(wide)
            if h == half:
                upper.append(jnp.where(inside, jnp.where(lane - off >= sub, done, 0.0), jnp.where(lane >= off + WIDE, wide, 0.0)))
                solved.append(jnp.where(inside, moved, jnp.where(lane < off, wide, 0.0)))
            else:
                upper.append(wide if h > half else zero)
                solved.append(wide if h < half else zero)
        upper, solved = jnp.concatenate(upper, axis=1), jnp.concatenate(solved, axis=1)
        u_ref[b0:stop] = upper
        x_ref[b0:stop] = solved
        if stop < order:
            eliminate_below(t_ref, upper, solved, stop)


def wall_diff(plane, count):
    total = jnp.zeros((count, plane.shape[1]), jnp.float32)
    for k, weight in zip((1, 2, 3), COEFS):
        total = total + weight * (plane[3 + k : 3 + k + count] - plane[3 - k : 3 - k + count])
    return total


def span_diff(band, edges):
    past, before = edges
    cells = band.shape[1]
    lane = lax.broadcasted_iota(jnp.int32, band.shape, 1)
    total = jnp.zeros(band.shape, jnp.float32)
    for k, weight in zip((1, 2, 3), COEFS):
        ahead = pltpu.roll(jnp.where(lane < k, past, band), cells - k, 1)
        behind = pltpu.roll(jnp.where(lane >= cells - k, before, band), k, 1)
        total = total + weight * (ahead - behind)
    return total


def stream_diff(planes, at):
    total = jnp.zeros(planes[0].shape, jnp.float32)
    for k, weight in zip((1, 2, 3), COEFS):
        total = total + weight * (planes[at + k] - planes[at - k])
    return total


def span_edges(rim_ref, which, turn_ref):
    snaps, slabs, _, _, rows = rim_ref.shape
    groups = [(s, i) for s in range(snaps) for i in range(slabs)]
    room = turn_ref.shape[0]
    edges = {}
    for start in range(0, len(groups), room // 8):
        some = groups[start : start + room // 8]
        turn_ref[...] = jnp.zeros_like(turn_ref)
        for g, (s, i) in enumerate(some):
            for at, entry in enumerate((3, 4, 5, None, None, 0, 1, 2)):
                if entry is not None:
                    turn_ref[8 * g + at : 8 * g + at + 1, :rows] = rim_ref[s, i, entry, which : which + 1, :]
        turned = turn_ref[...].T[:rows]
        for g, key in enumerate(some):
            edges[key] = (
                pltpu.roll(turned, (room - 8 * g) % room, 1),
                pltpu.roll(turned, (room - 8 - 8 * g) % room, 1),
            )
    return edges


def gain_matrix(omega, rows):
    snaps, rank = omega.shape
    high = omega.astype(jnp.bfloat16).astype(jnp.float32)
    low = omega - high
    pieces = [jnp.broadcast_to(part[s : s + 1], (rows, rank)) for part in (high, high, low) for s in range(snaps)]
    depth = 3 * snaps * rows
    pieces.append(jnp.zeros((-depth % 128, rank), jnp.float32))
    return jnp.concatenate(pieces, axis=0).astype(jnp.bfloat16)


def update_block(vort, right, new_ref, acc_ref):
    rows, cells, rank = new_ref.shape
    high = [v.astype(jnp.bfloat16).astype(jnp.float32) for v in vort]
    low = [v - h for v, h in zip(vort, high)]
    depth = right.shape[0]
    rest = jnp.zeros((depth - 3 * rows * len(vort), cells), jnp.float32)
    turned = jnp.concatenate(high + low + high + [rest], axis=0).T.astype(jnp.bfloat16)
    lane = lax.broadcasted_iota(jnp.int32, (1, depth), 1)
    for y in range(rows):
        mask = jnp.where(lax.rem(lane, rows) == y, 1.0, 0.0).astype(jnp.bfloat16)
        gain = jnp.dot(turned * mask, right, preferred_element_type=jnp.float32)
        new_ref[y] = (new_ref[y].astype(jnp.float32) + gain).astype(jnp.bfloat16)
    block = new_ref[...].reshape(rows * cells, rank)
    acc_ref[...] += lax.dot_general(block, block, (((0,), (0,)), ((), ())), preferred_element_type=jnp.float32)


def first_component_kernel(
    vel_in, rim_in, omega_in, old_ref,
    x_ref, y_ref, z_ref, gram_ref, vel_ref, rim_ref, omega_ref, turn_ref, small_sems, sems,
):
    small = [
        pltpu.make_async_copy(source, target, small_sems.at[n])
        for n, (source, target) in enumerate(((rim_in, rim_ref), (omega_in, omega_ref), (vel_in, vel_ref)))
    ]
    for copy in small:
        copy.start()
    snaps, _, slabs, height, _ = vel_ref.shape
    rows = height - 6
    copies = [
        [pltpu.make_async_copy(old_ref.at[c, i], new_ref.at[i], sems.at[c, i]) for i in range(slabs)]
        for c, new_ref in enumerate((x_ref, y_ref, z_ref))
    ]
    for row in copies:
        for copy in row:
            copy.start()
    gram_ref[...] = jnp.zeros_like(gram_ref)
    for copy in small:
        copy.wait()
    right = gain_matrix(omega_ref[...], rows)
    edges = span_edges(rim_ref, 1, turn_ref)
    for i in range(slabs):
        vort = [
            wall_diff(vel_ref[s, 2, i], rows) - span_diff(vel_ref[s, 1, i, 3 : 3 + rows], edges[s, i])
            for s in range(snaps)
        ]
        copies[0][i].wait()
        update_block(vort, right, x_ref.at[i], gram_ref)
    for row in copies[1:]:
        for copy in row:
            copy.wait()


def pack(gram_ref, first, keep_ref, send_ref):
    half = gram_ref.shape[0] // 2
    row = lax.broadcasted_iota(jnp.int32, (half, half), 0)
    col = lax.broadcasted_iota(jnp.int32, (half, half), 1)
    low = gram_ref[half:, half:]
    mixed = jnp.where(row <= col, gram_ref[:half, :half], low)
    diag = jnp.sum(jnp.where(row == col, low, 0.0), axis=0, keepdims=True)
    packed = jnp.concatenate([gram_ref[:half, half:], mixed], axis=1)
    part = half // 2
    extra = jnp.broadcast_to(jnp.concatenate([diag, diag], axis=1), (8, 2 * half))
    upper, lower = packed[:part], packed[part:]
    keep_ref[:part] = jnp.where(first, upper, lower)
    send_ref[:part] = jnp.where(first, lower, upper)
    keep_ref[part:] = extra
    send_ref[part:] = extra


def other_components_kernel(
    parity_ref, vel_ref, rim_ref, behind_ref, ahead_ref, omega_ref, start_ref, old_y_ref, old_z_ref,
    y_ref, z_ref, keep_ref, send_ref, wide_ref, gram_ref, turn_ref,
):
    del old_y_ref, old_z_ref
    snaps, _, slabs, height, _ = vel_ref.shape
    rows = height - 6
    gram_ref[...] = start_ref[...]
    right = gain_matrix(omega_ref[...], rows)
    edges = span_edges(rim_ref, 0, turn_ref)
    for s in range(snaps):
        for c in range(2):
            for k in range(3):
                at = ((s * 2 + c) * 3 + k) * rows
                wide_ref[s, c, k] = behind_ref[at : at + rows]
                wide_ref[s, c, 3 + slabs + k] = ahead_ref[at : at + rows]
            for i in range(slabs):
                wide_ref[s, c, 3 + i] = vel_ref[s, 1 + c, i, 3 : 3 + rows]
    for i in range(slabs):
        for c, new_ref in enumerate((y_ref, z_ref)):
            vort = []
            for s in range(snaps):
                along = stream_diff([wide_ref[s, 1 - c, i + k] for k in range(7)], 3)
                if c == 0:
                    vort.append(span_diff(vel_ref[s, 0, i, 3 : 3 + rows], edges[s, i]) - along)
                else:
                    vort.append(along - wall_diff(vel_ref[s, 0, i], rows))
            update_block(vort, right, new_ref.at[i], gram_ref)
    pack(gram_ref, parity_ref[0] == 0, keep_ref, send_ref)


def unpack(packed, part_diag, work_ref):
    half = packed.shape[0]
    cross, mixed = packed[:, :half], packed[:, half:]
    row = lax.broadcasted_iota(jnp.int32, (half, half), 0)
    col = lax.broadcasted_iota(jnp.int32, (half, half), 1)
    turned = mixed.T
    diag = jnp.broadcast_to(part_diag[:, :half], (half, half))
    work_ref[:half, :half] = jnp.where(row <= col, mixed, turned)
    work_ref[:half, half:] = cross
    work_ref[half:, :half] = cross.T
    work_ref[half:, half:] = jnp.where(row > col, mixed, jnp.where(row < col, turned, diag))


def basis_kernel(
    scale, parity_ref, mine_ref, other_ref, x_ref, y_ref, z_ref, upper_ref, basis_ref,
    work_ref, solved_ref, block_ref, stage_ref, sems,
):
    order = work_ref.shape[0]
    part = order // 4
    first = parity_ref[0] == 0
    mine, other = mine_ref[...] * scale, other_ref[...] * scale
    top, bottom = jnp.where(first, mine[:part], other[:part]), jnp.where(first, other[:part], mine[:part])
    unpack(jnp.concatenate([top, bottom], axis=0), mine[part : part + 1], work_ref)
    factor_invert(work_ref, upper_ref, solved_ref, block_ref)
    inverse = solved_ref[...].T.astype(jnp.bfloat16)
    copies = []
    for c, sketch_ref in enumerate((x_ref, y_ref, z_ref)):
        slabs, rows, cells, rank = sketch_ref.shape
        for i in range(slabs):
            block = sketch_ref[i].reshape(rows * cells, rank)
            product = jnp.dot(block, inverse, preferred_element_type=jnp.float32)
            stage_ref[c, i] = product.astype(jnp.bfloat16).reshape(rows, cells, rank)
            copy = pltpu.make_async_copy(stage_ref.at[c, i], basis_ref.at[c, i], sems.at[c, i])
            copy.start()
            copies.append(copy)
    for copy in copies:
        copy.wait()


def local(velocity, span_rim, sketch_old, omega):
    snaps, _, slabs, height, cells = velocity.shape
    rows = height - 6
    rank = omega.shape[1]
    count = lax.axis_size("gx")
    limit = pltpu.CompilerParams(vmem_limit_bytes=24 << 20)
    place = lax.axis_index("gx")
    parity = (place % 2).reshape(1)
    band = velocity[:, 1:3, :, 3 : 3 + rows]
    tail = band[:, :, slabs - 3 :].reshape(-1, cells)
    head = band[:, :, :3].reshape(-1, cells)
    behind = lax.ppermute(tail, "gx", [(i, (i + 1) % count) for i in range(count)])
    ahead = lax.ppermute(head, "gx", [((i + 1) % count, i) for i in range(count)])
    rim = span_rim.transpose(0, 2, 4, 1, 3)
    block = (slabs, rows, cells, rank)
    square = jax.ShapeDtypeStruct((rank, rank), jnp.float32)
    held = pltpu.VMEM(block, jnp.bfloat16)
    inputs = [velocity, rim, omega, sketch_old]
    sketch_x, raw_y, raw_z, gram, near_vel, near_rim, near_omega = pl.pallas_call(
        first_component_kernel,
        out_shape=[held, held, held, square] + [pltpu.VMEM(x.shape, x.dtype) for x in inputs[:3]],
        in_specs=[IN_HBM] * 4,
        out_specs=[IN_VMEM] * 7,
        scratch_shapes=[
            pltpu.VMEM((128, 128), jnp.float32),
            pltpu.SemaphoreType.DMA((3,)),
            pltpu.SemaphoreType.DMA((3, slabs)),
        ],
        compiler_params=limit,
    )(*(pltpu.with_memory_space_constraint(x, pltpu.HBM) for x in inputs))
    piece = jax.ShapeDtypeStruct((rank // 4 + 8, rank), jnp.float32)
    sketch_y, sketch_z, keep, send = pl.pallas_call(
        other_components_kernel,
        out_shape=[held, held, piece, piece],
        in_specs=[IN_SMEM] + [IN_VMEM] * 8,
        out_specs=[IN_VMEM] * 4,
        scratch_shapes=[
            pltpu.VMEM((snaps, 2, slabs + 6, rows, cells), jnp.float32),
            pltpu.VMEM((rank, rank), jnp.float32),
            pltpu.VMEM((128, 128), jnp.float32),
        ],
        input_output_aliases={7: 0, 8: 1},
        compiler_params=limit,
    )(parity, near_vel, near_rim, behind, ahead, near_omega, gram, raw_y, raw_z)
    swap = lambda k: [(i, i ^ k) for i in range(count)]
    total = keep + lax.ppermute(send, "gx", swap(1))
    step = 2
    while step < count:
        total = total + lax.ppermute(total, "gx", swap(step))
        step *= 2
    other = lax.ppermute(total, "gx", swap(1))
    entries = 3 * slabs * rows * cells * count
    factor, basis = pl.pallas_call(
        functools.partial(basis_kernel, 1.0 / entries),
        out_shape=[square, jax.ShapeDtypeStruct((3, *block), jnp.bfloat16)],
        in_specs=[IN_SMEM] + [IN_VMEM] * 5,
        out_specs=[IN_VMEM, IN_HBM],
        scratch_shapes=[
            pltpu.VMEM((rank, rank), jnp.float32),
            pltpu.VMEM((rank, rank), jnp.float32),
            pltpu.VMEM((WIDE, 128), jnp.float32),
            pltpu.VMEM((3, *block), jnp.bfloat16),
            pltpu.SemaphoreType.DMA((3, slabs)),
        ],
        compiler_params=limit,
    )(parity, total, other, sketch_x, sketch_y, sketch_z)
    return basis, factor


def solution(mesh):
    in_specs = (
        P(None, None, ("rec", "gx"), None, None),
        P(None, None, ("rec", "gx"), None, None),
        P(None, ("rec", "gx"), None, None, None),
        P(),
    )
    out_specs = (P(None, ("rec", "gx"), None, None, None), P("rec", None))
    return jax.shard_map(local, mesh=mesh, in_specs=in_specs, out_specs=out_specs, check_vma=False)
```

```python
import functools

import jax
import jax.numpy as jnp
from jax import lax
from jax.experimental import pallas as pl
from jax.experimental.pallas import tpu as pltpu
from jax.sharding import PartitionSpec as P

COEFS = (0.75, -0.15, 1.0 / 60.0)
IN_SMEM = pl.BlockSpec(memory_space=pltpu.SMEM)
IN_VMEM = pl.BlockSpec(memory_space=pltpu.VMEM)
IN_HBM = pl.BlockSpec(memory_space=pltpu.HBM)
WIDE = 64


def parts_of(x):
    high = x.astype(jnp.bfloat16).astype(jnp.float32)
    rest = x - high
    mid = rest.astype(jnp.bfloat16).astype(jnp.float32)
    return high, mid, rest - mid


def eliminate_below(t_ref, upper, solved, stop):
    order = t_ref.shape[0]
    col = lax.broadcasted_iota(jnp.int32, upper.shape, 1)
    v, w, y = parts_of(jnp.where(col < stop, solved, upper))
    right = jnp.concatenate([v, w, v, y, v, w], axis=0).astype(jnp.bfloat16)
    for base in range(stop // 128 * 128, order, 128):
        a, b, c = parts_of(upper[:, base : base + 128])
        left = jnp.concatenate([a, a, b, a, c, b], axis=0).astype(jnp.bfloat16)
        product = lax.dot_general(left, right, (((0,), (0,)), ((), ())), preferred_element_type=jnp.float32)
        for top in range(max(base, stop), base + 128, WIDE):
            kept = jnp.where((col >= stop - WIDE) & (col < stop), 0.0, t_ref[top : top + WIDE])
            t_ref[top : top + WIDE] = kept - product[top - base : top - base + WIDE]


def factor_block(w_ref, off):
    full = (8, 128)
    sub = lax.broadcasted_iota(jnp.int32, full, 0)
    for j0 in range(0, WIDE, 8):
        c0 = off + j0
        now = w_ref[j0 : j0 + 8]
        rows = [w_ref[pl.ds(j0 + i, 8, stride=0), :] for i in range(8)]
        a = {}
        for j in range(8):
            for i in range(j + 1):
                a[i, j] = jnp.broadcast_to(rows[i][:, c0 + j : c0 + j + 1], full)
        left, scaled, final = {}, {}, {}
        for k in range(0, 8, 2):
            n = k + 1
            top, mid, low = a[k, k], a[k, n], a[n, n]
            rdet = 1.0 / (top * low - mid * mid)
            for i in range(k + 2, 8):
                left[k, i] = (low * a[k, i] - mid * a[n, i]) * rdet
                left[n, i] = (top * a[n, i] - mid * a[k, i]) * rdet
            for i in range(k + 2, 8):
                for j in range(i, 8):
                    a[i, j] = a[i, j] - left[k, i] * a[k, j] - left[n, i] * a[n, j]
                rows[i] = rows[i] - left[k, i] * rows[k] - left[n, i] * rows[n]
            scaled[k] = (low * rows[k] - mid * rows[n]) * rdet
            scaled[n] = (top * rows[n] - mid * rows[k]) * rdet
            root = lax.rsqrt(top)
            ratio = mid * root * root
            final[k] = rows[k] * root
            final[n] = (rows[n] - ratio * rows[k]) * lax.rsqrt(low - mid * ratio)
        for k in reversed(range(8)):
            for i in reversed(range(k // 2 * 2 + 2, 8)):
                scaled[k] = scaled[k] - left[k, i] * scaled[i]
        for q in range(j0 + 8, WIDE, 8):
            old = w_ref[q : q + 8]
            rest = old
            for k in reversed(range(8)):
                rest = rest - jnp.broadcast_to(old[:, c0 + k : c0 + k + 1], full) * scaled[k]
            w_ref[q : q + 8] = rest
        out = final[0]
        for k in range(1, 8):
            out = jnp.where(sub == k, final[k], out)
        w_ref[j0 : j0 + 8] = out


def factor_invert(t_ref, u_ref, x_ref, w_ref):
    order = t_ref.shape[0]
    lane = lax.broadcasted_iota(jnp.int32, (WIDE, 128), 1)
    sub = lax.broadcasted_iota(jnp.int32, (WIDE, 128), 0)
    for b0 in range(0, order, WIDE):
        stop = b0 + WIDE
        half, off = b0 // 128, b0 % 128
        inside = (lane >= off) & (lane < off + WIDE)
        here = slice(128 * half, 128 * half + 128)
        w_ref[...] = jnp.where(inside, t_ref[b0:stop, here], jnp.where(lane == sub + (WIDE - off), 1.0, 0.0))
        factor_block(w_ref, off)
        done = w_ref[...]
        moved = pltpu.roll(done, 64, 1)
        low, high = (moved, done) if off == 0 else (done, moved)
        x1, x2, x3 = parts_of(low)
        y1, y2, _ = parts_of(high)
        r1, r2, r3 = parts_of(t_ref[b0:stop])
        pair = lambda p, q: jnp.where(lane < WIDE, p, q)
        first = jnp.concatenate([pair(x1, y1), pair(x2, y1), pair(x3, y2)], axis=1).astype(jnp.bfloat16)
        second = jnp.concatenate([r1, r2, r1, r3, r1, r2], axis=0).astype(jnp.bfloat16)
        rows = jnp.dot(first, second, preferred_element_type=jnp.float32)
        upper, solved = [], []
        for h in range(order // 128):
            wide = rows[:, 128 * h : 128 * h + 128]
            zero = jnp.zeros_like(wide)
            if h == half:
                upper.append(jnp.where(inside, jnp.where(lane - off >= sub, done, 0.0), jnp.where(lane >= off + WIDE, wide, 0.0)))
                solved.append(jnp.where(inside, moved, jnp.where(lane < off, wide, 0.0)))
            else:
                upper.append(wide if h > half else zero)
                solved.append(wide if h < half else zero)
        upper, solved = jnp.concatenate(upper, axis=1), jnp.concatenate(solved, axis=1)
        u_ref[b0:stop] = upper
        x_ref[b0:stop] = solved
        if stop < order:
            eliminate_below(t_ref, upper, solved, stop)


def wall_diff(plane, count):
    total = jnp.zeros((count, plane.shape[1]), jnp.float32)
    for k, weight in zip((1, 2, 3), COEFS):
        total = total + weight * (plane[3 + k : 3 + k + count] - plane[3 - k : 3 - k + count])
    return total


def span_diff(band, edges):
    past, before = edges
    cells = band.shape[1]
    lane = lax.broadcasted_iota(jnp.int32, band.shape, 1)
    total = jnp.zeros(band.shape, jnp.float32)
    for k, weight in zip((1, 2, 3), COEFS):
        ahead = pltpu.roll(jnp.where(lane < k, past, band), cells - k, 1)
        behind = pltpu.roll(jnp.where(lane >= cells - k, before, band), k, 1)
        total = total + weight * (ahead - behind)
    return total


def stream_diff(planes, at):
    total = jnp.zeros(planes[0].shape, jnp.float32)
    for k, weight in zip((1, 2, 3), COEFS):
        total = total + weight * (planes[at + k] - planes[at - k])
    return total


def span_edges(rim_ref, which, turn_ref):
    snaps, slabs, _, _, rows = rim_ref.shape
    groups = [(s, i) for s in range(snaps) for i in range(slabs)]
    room = turn_ref.shape[0]
    edges = {}
    for start in range(0, len(groups), room // 8):
        some = groups[start : start + room // 8]
        turn_ref[...] = jnp.zeros_like(turn_ref)
        for g, (s, i) in enumerate(some):
            for at, entry in enumerate((3, 4, 5, None, None, 0, 1, 2)):
                if entry is not None:
                    turn_ref[8 * g + at : 8 * g + at + 1, :rows] = rim_ref[s, i, entry, which : which + 1, :]
        turned = turn_ref[...].T[:rows]
        for g, key in enumerate(some):
            edges[key] = (
                pltpu.roll(turned, (room - 8 * g) % room, 1),
                pltpu.roll(turned, (room - 8 - 8 * g) % room, 1),
            )
    return edges


def gain_matrix(omega, rows):
    snaps, rank = omega.shape
    high = omega.astype(jnp.bfloat16).astype(jnp.float32)
    low = omega - high
    pieces = [jnp.broadcast_to(part[s : s + 1], (rows, rank)) for part in (high, high, low) for s in range(snaps)]
    depth = 3 * snaps * rows
    pieces.append(jnp.zeros((-depth % 128, rank), jnp.float32))
    return jnp.concatenate(pieces, axis=0).astype(jnp.bfloat16)


def update_block(vort, right, new_ref, acc_ref):
    rows, cells, rank = new_ref.shape
    high = [v.astype(jnp.bfloat16).astype(jnp.float32) for v in vort]
    low = [v - h for v, h in zip(vort, high)]
    depth = right.shape[0]
    rest = jnp.zeros((depth - 3 * rows * len(vort), cells), jnp.float32)
    turned = jnp.concatenate(high + low + high + [rest], axis=0).T.astype(jnp.bfloat16)
    lane = lax.broadcasted_iota(jnp.int32, (1, depth), 1)
    for y in range(rows):
        mask = jnp.where(lax.rem(lane, rows) == y, 1.0, 0.0).astype(jnp.bfloat16)
        gain = jnp.dot(turned * mask, right, preferred_element_type=jnp.float32)
        new_ref[y] = (new_ref[y].astype(jnp.float32) + gain).astype(jnp.bfloat16)
    block = new_ref[...].reshape(rows * cells, rank)
    acc_ref[...] += lax.dot_general(block, block, (((0,), (0,)), ((), ())), preferred_element_type=jnp.float32)


def start_kernel(vel_in, rim_in, omega_in, old_ref, band_ref, x_ref, vel_ref, rim_ref, omega_ref, small_sems, sems):
    snaps, _, slabs, height, _ = vel_ref.shape
    rows = height - 6
    copies = [
        pltpu.make_async_copy(source, target, small_sems.at[n])
        for n, (source, target) in enumerate(((vel_in, vel_ref), (rim_in, rim_ref), (omega_in, omega_ref)))
    ]
    copies += [pltpu.make_async_copy(old_ref.at[0, i], x_ref.at[i], sems.at[i]) for i in range(slabs)]
    for copy in copies:
        copy.start()
    copies[0].wait()
    for s in range(snaps):
        for c in range(2):
            for i in range(slabs):
                at = ((s * 2 + c) * slabs + i) * rows
                band_ref[at : at + rows] = vel_ref[s, 1 + c, i, 3 : 3 + rows]
    for copy in copies[1:]:
        copy.wait()


def first_component_kernel(
    vel_ref, rim_ref, omega_ref, old_x_ref, old_ref, x_ref, y_ref, z_ref, gram_ref, turn_ref, sems
):
    del old_x_ref
    snaps, _, slabs, height, _ = vel_ref.shape
    rows = height - 6
    copies = [
        pltpu.make_async_copy(old_ref.at[1 + c, i], new_ref.at[i], sems.at[c, i])
        for c, new_ref in enumerate((y_ref, z_ref))
        for i in range(slabs)
    ]
    for copy in copies:
        copy.start()
    gram_ref[...] = jnp.zeros_like(gram_ref)
    right = gain_matrix(omega_ref[...], rows)
    edges = span_edges(rim_ref, 1, turn_ref)
    for i in range(slabs):
        vort = [
            wall_diff(vel_ref[s, 2, i], rows) - span_diff(vel_ref[s, 1, i, 3 : 3 + rows], edges[s, i])
            for s in range(snaps)
        ]
        update_block(vort, right, x_ref.at[i], gram_ref)
    for copy in copies:
        copy.wait()


def pack(gram_ref, first, keep_ref, send_ref):
    half = gram_ref.shape[0] // 2
    row = lax.broadcasted_iota(jnp.int32, (half, half), 0)
    col = lax.broadcasted_iota(jnp.int32, (half, half), 1)
    low = gram_ref[half:, half:]
    mixed = jnp.where(row <= col, gram_ref[:half, :half], low)
    diag = jnp.sum(jnp.where(row == col, low, 0.0), axis=0, keepdims=True)
    packed = jnp.concatenate([gram_ref[:half, half:], mixed], axis=1)
    part = half // 2
    extra = jnp.broadcast_to(jnp.concatenate([diag, diag], axis=1), (8, 2 * half))
    upper, lower = packed[:part], packed[part:]
    keep_ref[:part] = jnp.where(first, upper, lower)
    send_ref[:part] = jnp.where(first, lower, upper)
    keep_ref[part:] = extra
    send_ref[part:] = extra


def other_components_kernel(
    parity_ref, vel_ref, rim_ref, inner_ref, outer_ref, omega_ref, start_ref, old_y_ref, old_z_ref,
    y_ref, z_ref, keep_ref, send_ref, wide_ref, gram_ref, turn_ref,
):
    del old_y_ref, old_z_ref
    snaps, _, slabs, height, _ = vel_ref.shape
    rows = height - 6
    gram_ref[...] = start_ref[...]
    right = gain_matrix(omega_ref[...], rows)
    edges = span_edges(rim_ref, 0, turn_ref)
    even = parity_ref[0] == 0
    for s in range(snaps):
        for c in range(2):
            for k in range(3):
                at = ((s * 2 + c) * 3 + k) * rows
                inner, outer = inner_ref[at : at + rows], outer_ref[at : at + rows]
                wide_ref[s, c, k] = jnp.where(even, outer, inner)
                wide_ref[s, c, 3 + slabs + k] = jnp.where(even, inner, outer)
            for i in range(slabs):
                wide_ref[s, c, 3 + i] = vel_ref[s, 1 + c, i, 3 : 3 + rows]
    for i in range(slabs):
        for c, new_ref in enumerate((y_ref, z_ref)):
            vort = []
            for s in range(snaps):
                along = stream_diff([wide_ref[s, 1 - c, i + k] for k in range(7)], 3)
                if c == 0:
                    vort.append(span_diff(vel_ref[s, 0, i, 3 : 3 + rows], edges[s, i]) - along)
                else:
                    vort.append(along - wall_diff(vel_ref[s, 0, i], rows))
            update_block(vort, right, new_ref.at[i], gram_ref)
    pack(gram_ref, even, keep_ref, send_ref)


def unpack(packed, part_diag, work_ref):
    half = packed.shape[0]
    cross, mixed = packed[:, :half], packed[:, half:]
    row = lax.broadcasted_iota(jnp.int32, (half, half), 0)
    col = lax.broadcasted_iota(jnp.int32, (half, half), 1)
    turned = mixed.T
    diag = jnp.broadcast_to(part_diag[:, :half], (half, half))
    work_ref[:half, :half] = jnp.where(row <= col, mixed, turned)
    work_ref[:half, half:] = cross
    work_ref[half:, :half] = cross.T
    work_ref[half:, half:] = jnp.where(row > col, mixed, jnp.where(row < col, turned, diag))


def basis_kernel(
    scale, parity_ref, mine_ref, other_ref, x_ref, y_ref, z_ref, factor_ref, basis_ref,
    work_ref, upper_ref, solved_ref, block_ref, stage_ref, factor_sem, sems,
):
    order = work_ref.shape[0]
    part = order // 4
    first = parity_ref[0] == 0
    mine, other = mine_ref[...] * scale, other_ref[...] * scale
    top, bottom = jnp.where(first, mine[:part], other[:part]), jnp.where(first, other[:part], mine[:part])
    unpack(jnp.concatenate([top, bottom], axis=0), mine[part : part + 1], work_ref)
    factor_invert(work_ref, upper_ref, solved_ref, block_ref)
    copies = [pltpu.make_async_copy(upper_ref, factor_ref, factor_sem)]
    copies[0].start()
    inverse = solved_ref[...].T.astype(jnp.bfloat16)
    for c, sketch_ref in enumerate((x_ref, y_ref, z_ref)):
        slabs, rows, cells, rank = sketch_ref.shape
        for i in range(slabs):
            block = sketch_ref[i].reshape(rows * cells, rank)
            product = jnp.dot(block, inverse, preferred_element_type=jnp.float32)
            stage_ref[c, i] = product.astype(jnp.bfloat16).reshape(rows, cells, rank)
            copy = pltpu.make_async_copy(stage_ref.at[c, i], basis_ref.at[c, i], sems.at[c, i])
            copy.start()
            copies.append(copy)
    for copy in copies:
        copy.wait()


def local(velocity, span_rim, sketch_old, omega):
    snaps, _, slabs, height, cells = velocity.shape
    rows = height - 6
    rank = omega.shape[1]
    count = lax.axis_size("gx")
    limit = pltpu.CompilerParams(vmem_limit_bytes=24 << 20)
    place = lax.axis_index("gx")
    parity = (place % 2).reshape(1)
    rim = span_rim.transpose(0, 2, 4, 1, 3)
    block = (slabs, rows, cells, rank)
    square = jax.ShapeDtypeStruct((rank, rank), jnp.float32)
    held = pltpu.VMEM(block, jnp.bfloat16)
    old = pltpu.with_memory_space_constraint(sketch_old, pltpu.HBM)
    small = [pltpu.with_memory_space_constraint(x, pltpu.HBM) for x in (velocity, rim, omega)]
    planes, raw_x, near_vel, near_rim, near_omega = pl.pallas_call(
        start_kernel,
        out_shape=[pltpu.VMEM((snaps * 2 * slabs * rows, cells), jnp.float32), held]
        + [pltpu.VMEM(x.shape, x.dtype) for x in (velocity, rim, omega)],
        in_specs=[IN_HBM] * 4,
        out_specs=[IN_VMEM] * 5,
        scratch_shapes=[pltpu.SemaphoreType.DMA((3,)), pltpu.SemaphoreType.DMA((slabs,))],
        compiler_params=limit,
    )(*small, old)
    inner, outer = planes, planes
    if slabs > 3:
        whole = planes.reshape(snaps * 2, slabs, rows, cells)
        head, tail = (x.reshape(-1, cells) for x in (whole[:, :3], whole[:, slabs - 3 :]))
        even = place % 2 == 0
        inner, outer = jnp.where(even, tail, head), jnp.where(even, head, tail)
    ring = lambda i: i % count
    outer = lax.ppermute(outer, "gx", [(i, ring(i + (1 if i % 2 else -1))) for i in range(count)])
    inner = lax.ppermute(inner, "gx", [(i, i ^ 1) for i in range(count)])
    sketch_x, raw_y, raw_z, gram = pl.pallas_call(
        first_component_kernel,
        out_shape=[held, held, held, square],
        in_specs=[IN_VMEM] * 4 + [IN_HBM],
        out_specs=[IN_VMEM] * 4,
        scratch_shapes=[pltpu.VMEM((128, 128), jnp.float32), pltpu.SemaphoreType.DMA((2, slabs))],
        input_output_aliases={3: 0},
        compiler_params=limit,
    )(near_vel, near_rim, near_omega, raw_x, old)
    piece = jax.ShapeDtypeStruct((rank // 4 + 8, rank), jnp.float32)
    sketch_y, sketch_z, keep, send = pl.pallas_call(
        other_components_kernel,
        out_shape=[held, held, piece, piece],
        in_specs=[IN_SMEM] + [IN_VMEM] * 8,
        out_specs=[IN_VMEM] * 4,
        scratch_shapes=[
            pltpu.VMEM((snaps, 2, slabs + 6, rows, cells), jnp.float32),
            pltpu.VMEM((rank, rank), jnp.float32),
            pltpu.VMEM((128, 128), jnp.float32),
        ],
        input_output_aliases={7: 0, 8: 1},
        compiler_params=limit,
    )(parity, near_vel, near_rim, inner, outer, near_omega, gram, raw_y, raw_z)
    swap = lambda k: [(i, i ^ k) for i in range(count)]
    total = keep + lax.ppermute(send, "gx", swap(1))
    step = 2
    while step < count:
        total = total + lax.ppermute(total, "gx", swap(step))
        step *= 2
    other = lax.ppermute(total, "gx", swap(1))
    entries = 3 * slabs * rows * cells * count
    factor, basis = pl.pallas_call(
        functools.partial(basis_kernel, 1.0 / entries),
        out_shape=[square, jax.ShapeDtypeStruct((3, *block), jnp.bfloat16)],
        in_specs=[IN_SMEM] + [IN_VMEM] * 5,
        out_specs=[IN_HBM, IN_HBM],
        scratch_shapes=[
            pltpu.VMEM((rank, rank), jnp.float32),
            pltpu.VMEM((rank, rank), jnp.float32),
            pltpu.VMEM((rank, rank), jnp.float32),
            pltpu.VMEM((WIDE, 128), jnp.float32),
            pltpu.VMEM((3, *block), jnp.bfloat16),
            pltpu.SemaphoreType.DMA,
            pltpu.SemaphoreType.DMA((3, slabs)),
        ],
        compiler_params=limit,
    )(parity, total, other, sketch_x, sketch_y, sketch_z)
    return basis, factor


def solution(mesh):
    in_specs = (
        P(None, None, ("rec", "gx"), None, None),
        P(None, None, ("rec", "gx"), None, None),
        P(None, ("rec", "gx"), None, None, None),
        P(),
    )
    out_specs = (P(None, ("rec", "gx"), None, None, None), P("rec", None))
    return jax.shard_map(local, mesh=mesh, in_specs=in_specs, out_specs=out_specs, check_vma=False)
```

```python
import functools

import jax
import jax.numpy as jnp
from jax import lax
from jax.experimental import pallas as pl
from jax.experimental.pallas import tpu as pltpu
from jax.sharding import PartitionSpec as P

COEFS = (0.75, -0.15, 1.0 / 60.0)
IN_SMEM = pl.BlockSpec(memory_space=pltpu.SMEM)
IN_VMEM = pl.BlockSpec(memory_space=pltpu.VMEM)
IN_HBM = pl.BlockSpec(memory_space=pltpu.HBM)
WIDE = 64


def parts_of(x):
    high = x.astype(jnp.bfloat16).astype(jnp.float32)
    rest = x - high
    mid = rest.astype(jnp.bfloat16).astype(jnp.float32)
    return high, mid, rest - mid


def eliminate_below(t_ref, upper, solved, stop):
    order = t_ref.shape[0]
    col = lax.broadcasted_iota(jnp.int32, upper.shape, 1)
    v, w, y = parts_of(jnp.where(col < stop, solved, upper))
    right = jnp.concatenate([v, w, v, y, v, w], axis=0).astype(jnp.bfloat16)
    for base in range(stop // 128 * 128, order, 128):
        a, b, c = parts_of(upper[:, base : base + 128])
        left = jnp.concatenate([a, a, b, a, c, b], axis=0).astype(jnp.bfloat16)
        product = lax.dot_general(left, right, (((0,), (0,)), ((), ())), preferred_element_type=jnp.float32)
        for top in range(max(base, stop), base + 128, WIDE):
            kept = jnp.where((col >= stop - WIDE) & (col < stop), 0.0, t_ref[top : top + WIDE])
            t_ref[top : top + WIDE] = kept - product[top - base : top - base + WIDE]


def factor_block(w_ref, off, spare):
    full = (8, 128)
    sub = lax.broadcasted_iota(jnp.int32, full, 0)
    for j0 in range(0, WIDE, 8):
        c0 = off + j0
        now = w_ref[j0 : j0 + 8]
        rows = [w_ref[pl.ds(j0 + i, 8, stride=0), :] for i in range(8)]
        a = {}
        for j in range(8):
            for i in range(j + 1):
                a[i, j] = jnp.broadcast_to(rows[i][:, c0 + j : c0 + j + 1], full)
        left, scaled, final = {}, {}, {}
        for k in range(0, 8, 2):
            n = k + 1
            top, mid, low = a[k, k], a[k, n], a[n, n]
            rdet = 1.0 / (top * low - mid * mid)
            for i in range(k + 2, 8):
                left[k, i] = (low * a[k, i] - mid * a[n, i]) * rdet
                left[n, i] = (top * a[n, i] - mid * a[k, i]) * rdet
            for i in range(k + 2, 8):
                for j in range(i, 8):
                    a[i, j] = a[i, j] - left[k, i] * a[k, j] - left[n, i] * a[n, j]
                rows[i] = rows[i] - left[k, i] * rows[k] - left[n, i] * rows[n]
            scaled[k] = (low * rows[k] - mid * rows[n]) * rdet
            scaled[n] = (top * rows[n] - mid * rows[k]) * rdet
            root = lax.rsqrt(top)
            ratio = mid * root * root
            final[k] = rows[k] * root
            final[n] = (rows[n] - ratio * rows[k]) * lax.rsqrt(low - mid * ratio)
        for k in reversed(range(8)):
            for i in reversed(range(k // 2 * 2 + 2, 8)):
                scaled[k] = scaled[k] - left[k, i] * scaled[i]
        for q in range(j0 + 8, WIDE, 8):
            old = w_ref[q : q + 8]
            rest = old
            for k in reversed(range(8)):
                rest = rest - jnp.broadcast_to(old[:, c0 + k : c0 + k + 1], full) * scaled[k]
            w_ref[q : q + 8] = rest
        out = final[0]
        for k in range(1, 8):
            out = jnp.where(sub == k, final[k], out)
        w_ref[j0 : j0 + 8] = out
        if spare:
            spare.pop(0)()


def factor_invert(t_ref, u_ref, x_ref, w_ref, spare):
    order = t_ref.shape[0]
    lane = lax.broadcasted_iota(jnp.int32, (WIDE, 128), 1)
    sub = lax.broadcasted_iota(jnp.int32, (WIDE, 128), 0)
    for b0 in range(0, order, WIDE):
        stop = b0 + WIDE
        half, off = b0 // 128, b0 % 128
        inside = (lane >= off) & (lane < off + WIDE)
        here = slice(128 * half, 128 * half + 128)
        w_ref[...] = jnp.where(inside, t_ref[b0:stop, here], jnp.where(lane == sub + (WIDE - off), 1.0, 0.0))
        factor_block(w_ref, off, spare if b0 >= order // 2 else [])
        done = w_ref[...]
        moved = pltpu.roll(done, 64, 1)
        low, high = (moved, done) if off == 0 else (done, moved)
        x1, x2, x3 = parts_of(low)
        y1, y2, _ = parts_of(high)
        r1, r2, r3 = parts_of(t_ref[b0:stop])
        pair = lambda p, q: jnp.where(lane < WIDE, p, q)
        first = jnp.concatenate([pair(x1, y1), pair(x2, y1), pair(x3, y2)], axis=1).astype(jnp.bfloat16)
        second = jnp.concatenate([r1, r2, r1, r3, r1, r2], axis=0).astype(jnp.bfloat16)
        rows = jnp.dot(first, second, preferred_element_type=jnp.float32)
        upper, solved = [], []
        for h in range(order // 128):
            wide = rows[:, 128 * h : 128 * h + 128]
            zero = jnp.zeros_like(wide)
            if h == half:
                upper.append(jnp.where(inside, jnp.where(lane - off >= sub, done, 0.0), jnp.where(lane >= off + WIDE, wide, 0.0)))
                solved.append(jnp.where(inside, moved, jnp.where(lane < off, wide, 0.0)))
            else:
                upper.append(wide if h > half else zero)
                solved.append(wide if h < half else zero)
        upper, solved = jnp.concatenate(upper, axis=1), jnp.concatenate(solved, axis=1)
        u_ref[b0:stop] = upper
        x_ref[b0:stop] = solved
        if stop < order:
            eliminate_below(t_ref, upper, solved, stop)


def wall_diff(plane, count):
    total = jnp.zeros((count, plane.shape[1]), jnp.float32)
    for k, weight in zip((1, 2, 3), COEFS):
        total = total + weight * (plane[3 + k : 3 + k + count] - plane[3 - k : 3 - k + count])
    return total


def span_diff(band, edges):
    past, before = edges
    cells = band.shape[1]
    lane = lax.broadcasted_iota(jnp.int32, band.shape, 1)
    total = jnp.zeros(band.shape, jnp.float32)
    for k, weight in zip((1, 2, 3), COEFS):
        ahead = pltpu.roll(jnp.where(lane < k, past, band), cells - k, 1)
        behind = pltpu.roll(jnp.where(lane >= cells - k, before, band), k, 1)
        total = total + weight * (ahead - behind)
    return total


def stream_diff(planes, at):
    total = jnp.zeros(planes[0].shape, jnp.float32)
    for k, weight in zip((1, 2, 3), COEFS):
        total = total + weight * (planes[at + k] - planes[at - k])
    return total


def span_edges(rim_ref, which, turn_ref):
    snaps, slabs, _, _, rows = rim_ref.shape
    groups = [(s, i) for s in range(snaps) for i in range(slabs)]
    room = turn_ref.shape[0]
    edges = {}
    for start in range(0, len(groups), room // 8):
        some = groups[start : start + room // 8]
        turn_ref[...] = jnp.zeros_like(turn_ref)
        for g, (s, i) in enumerate(some):
            for at, entry in enumerate((3, 4, 5, None, None, 0, 1, 2)):
                if entry is not None:
                    turn_ref[8 * g + at : 8 * g + at + 1, :rows] = rim_ref[s, i, entry, which : which + 1, :]
        turned = turn_ref[...].T[:rows]
        for g, key in enumerate(some):
            edges[key] = (
                pltpu.roll(turned, (room - 8 * g) % room, 1),
                pltpu.roll(turned, (room - 8 - 8 * g) % room, 1),
            )
    return edges


def gain_matrix(omega, rows):
    snaps, rank = omega.shape
    high = omega.astype(jnp.bfloat16).astype(jnp.float32)
    low = omega - high
    pieces = [jnp.broadcast_to(part[s : s + 1], (rows, rank)) for part in (high, high, low) for s in range(snaps)]
    depth = 3 * snaps * rows
    pieces.append(jnp.zeros((-depth % 128, rank), jnp.float32))
    return jnp.concatenate(pieces, axis=0).astype(jnp.bfloat16)


def update_block(vort, right, new_ref, acc_ref):
    rows, cells, rank = new_ref.shape
    high = [v.astype(jnp.bfloat16).astype(jnp.float32) for v in vort]
    low = [v - h for v, h in zip(vort, high)]
    depth = right.shape[0]
    rest = jnp.zeros((depth - 3 * rows * len(vort), cells), jnp.float32)
    turned = jnp.concatenate(high + low + high + [rest], axis=0).T.astype(jnp.bfloat16)
    lane = lax.broadcasted_iota(jnp.int32, (1, depth), 1)
    for y in range(rows):
        mask = jnp.where(lax.rem(lane, rows) == y, 1.0, 0.0).astype(jnp.bfloat16)
        gain = jnp.dot(turned * mask, right, preferred_element_type=jnp.float32)
        new_ref[y] = (new_ref[y].astype(jnp.float32) + gain).astype(jnp.bfloat16)
    block = new_ref[...].reshape(rows * cells, rank)
    acc_ref[...] += lax.dot_general(block, block, (((0,), (0,)), ((), ())), preferred_element_type=jnp.float32)


def start_kernel(vel_in, rim_in, omega_in, band_ref, vel_ref, rim_ref, omega_ref, sems):
    snaps, _, slabs, height, _ = vel_ref.shape
    rows = height - 6
    copies = [
        pltpu.make_async_copy(source, target, sems.at[n])
        for n, (source, target) in enumerate(((vel_in, vel_ref), (rim_in, rim_ref), (omega_in, omega_ref)))
    ]
    for copy in copies:
        copy.start()
    copies[0].wait()
    for s in range(snaps):
        for c in range(2):
            for i in range(slabs):
                at = ((s * 2 + c) * slabs + i) * rows
                band_ref[at : at + rows] = vel_ref[s, 1 + c, i, 3 : 3 + rows]
    for copy in copies[1:]:
        copy.wait()


def first_component_kernel(
    vel_ref, rim_ref, omega_ref, old_ref, x_ref, y_ref, z_ref, gram_ref, turn_ref, sems
):
    snaps, _, slabs, height, _ = vel_ref.shape
    rows = height - 6
    copies = [
        pltpu.make_async_copy(old_ref.at[c, i], new_ref.at[i], sems.at[c, i])
        for c, new_ref in enumerate((x_ref, y_ref, z_ref))
        for i in range(slabs)
    ]
    for copy in copies:
        copy.start()
    gram_ref[...] = jnp.zeros_like(gram_ref)
    right = gain_matrix(omega_ref[...], rows)
    edges = span_edges(rim_ref, 1, turn_ref)
    for i in range(slabs):
        vort = [
            wall_diff(vel_ref[s, 2, i], rows) - span_diff(vel_ref[s, 1, i, 3 : 3 + rows], edges[s, i])
            for s in range(snaps)
        ]
        copies[i].wait()
        update_block(vort, right, x_ref.at[i], gram_ref)
    for copy in copies[slabs:]:
        copy.wait()


def pack(gram_ref, first, keep_ref, send_ref):
    half = gram_ref.shape[0] // 2
    row = lax.broadcasted_iota(jnp.int32, (half, half), 0)
    col = lax.broadcasted_iota(jnp.int32, (half, half), 1)
    low = gram_ref[half:, half:]
    mixed = jnp.where(row <= col, gram_ref[:half, :half], low)
    diag = jnp.sum(jnp.where(row == col, low, 0.0), axis=0, keepdims=True)
    packed = jnp.concatenate([gram_ref[:half, half:], mixed], axis=1)
    part = half // 2
    extra = jnp.broadcast_to(jnp.concatenate([diag, diag], axis=1), (8, 2 * half))
    upper, lower = packed[:part], packed[part:]
    keep_ref[:part] = jnp.where(first, upper, lower)
    send_ref[:part] = jnp.where(first, lower, upper)
    keep_ref[part:] = extra
    send_ref[part:] = extra


def other_components_kernel(
    parity_ref, vel_ref, rim_ref, inner_ref, outer_ref, omega_ref, start_ref, old_y_ref, old_z_ref,
    y_ref, z_ref, keep_ref, send_ref, wide_ref, gram_ref, turn_ref,
):
    del old_y_ref, old_z_ref
    snaps, _, slabs, height, _ = vel_ref.shape
    rows = height - 6
    gram_ref[...] = start_ref[...]
    right = gain_matrix(omega_ref[...], rows)
    edges = span_edges(rim_ref, 0, turn_ref)
    even = parity_ref[0] == 0
    for s in range(snaps):
        for c in range(2):
            for k in range(3):
                at = ((s * 2 + c) * 3 + k) * rows
                inner, outer = inner_ref[at : at + rows], outer_ref[at : at + rows]
                wide_ref[s, c, k] = jnp.where(even, outer, inner)
                wide_ref[s, c, 3 + slabs + k] = jnp.where(even, inner, outer)
            for i in range(slabs):
                wide_ref[s, c, 3 + i] = vel_ref[s, 1 + c, i, 3 : 3 + rows]
    for i in range(slabs):
        for c, new_ref in enumerate((y_ref, z_ref)):
            vort = []
            for s in range(snaps):
                along = stream_diff([wide_ref[s, 1 - c, i + k] for k in range(7)], 3)
                if c == 0:
                    vort.append(span_diff(vel_ref[s, 0, i, 3 : 3 + rows], edges[s, i]) - along)
                else:
                    vort.append(along - wall_diff(vel_ref[s, 0, i], rows))
            update_block(vort, right, new_ref.at[i], gram_ref)
    pack(gram_ref, even, keep_ref, send_ref)


def unpack(packed, part_diag, work_ref):
    half = packed.shape[0]
    cross, mixed = packed[:, :half], packed[:, half:]
    row = lax.broadcasted_iota(jnp.int32, (half, half), 0)
    col = lax.broadcasted_iota(jnp.int32, (half, half), 1)
    turned = mixed.T
    diag = jnp.broadcast_to(part_diag[:, :half], (half, half))
    work_ref[:half, :half] = jnp.where(row <= col, mixed, turned)
    work_ref[:half, half:] = cross
    work_ref[half:, :half] = cross.T
    work_ref[half:, half:] = jnp.where(row > col, mixed, jnp.where(row < col, turned, diag))


def basis_kernel(
    scale, parity_ref, mine_ref, other_ref, x_ref, y_ref, z_ref, factor_ref, basis_ref,
    work_ref, upper_ref, solved_ref, block_ref, low_ref, high_ref, factor_sem, sems,
):
    order = work_ref.shape[0]
    part = order // 4
    first = parity_ref[0] == 0
    mine, other = mine_ref[...] * scale, other_ref[...] * scale
    top, bottom = jnp.where(first, mine[:part], other[:part]), jnp.where(first, other[:part], mine[:part])
    unpack(jnp.concatenate([top, bottom], axis=0), mine[part : part + 1], work_ref)
    half = order // 2
    blocks = [(c, i, ref) for c, ref in enumerate((x_ref, y_ref, z_ref)) for i in range(ref.shape[0])]
    copies = []

    def multiply(c, i, sketch_ref, stage_ref, side, get_inverse):
        _, rows, cells, _ = sketch_ref.shape
        block = sketch_ref[i, :, :, : half * (side + 1)].reshape(rows * cells, half * (side + 1))
        product = jnp.dot(block, get_inverse(), preferred_element_type=jnp.float32)
        stage_ref[c, i] = product.astype(jnp.bfloat16).reshape(rows, cells, half)
        columns = pl.ds(half * side, half)
        copy = pltpu.make_async_copy(
            stage_ref.at[c, i], basis_ref.at[c, i, :, :, columns], sems.at[side, c, i]
        )
        copy.start()
        copies.append(copy)

    first_inverse = lambda: solved_ref[:half, :half].T.astype(jnp.bfloat16)
    spare = [functools.partial(multiply, *block, low_ref, 0, first_inverse) for block in blocks]
    factor_invert(work_ref, upper_ref, solved_ref, block_ref, spare)
    for piece in spare:
        piece()
    factor_copy = pltpu.make_async_copy(upper_ref, factor_ref, factor_sem)
    factor_copy.start()
    inverse = solved_ref[half:].T.astype(jnp.bfloat16)
    for block in blocks:
        multiply(*block, high_ref, 1, lambda: inverse)
    for copy in [factor_copy] + copies:
        copy.wait()


def local(velocity, span_rim, sketch_old, omega):
    snaps, _, slabs, height, cells = velocity.shape
    rows = height - 6
    rank = omega.shape[1]
    count = lax.axis_size("gx")
    limit = pltpu.CompilerParams(vmem_limit_bytes=24 << 20)
    place = lax.axis_index("gx")
    parity = (place % 2).reshape(1)
    rim = span_rim.transpose(0, 2, 4, 1, 3)
    block = (slabs, rows, cells, rank)
    square = jax.ShapeDtypeStruct((rank, rank), jnp.float32)
    held = pltpu.VMEM(block, jnp.bfloat16)
    old = pltpu.with_memory_space_constraint(sketch_old, pltpu.HBM)
    small = [pltpu.with_memory_space_constraint(x, pltpu.HBM) for x in (velocity, rim, omega)]
    planes, near_vel, near_rim, near_omega = pl.pallas_call(
        start_kernel,
        out_shape=[pltpu.VMEM((snaps * 2 * slabs * rows, cells), jnp.float32)]
        + [pltpu.VMEM(x.shape, x.dtype) for x in (velocity, rim, omega)],
        in_specs=[IN_HBM] * 3,
        out_specs=[IN_VMEM] * 4,
        scratch_shapes=[pltpu.SemaphoreType.DMA((3,))],
        compiler_params=limit,
    )(*small)
    inner, outer = planes, planes
    if slabs > 3:
        whole = planes.reshape(snaps * 2, slabs, rows, cells)
        head, tail = (x.reshape(-1, cells) for x in (whole[:, :3], whole[:, slabs - 3 :]))
        even = place % 2 == 0
        inner, outer = jnp.where(even, tail, head), jnp.where(even, head, tail)
    ring = lambda i: i % count
    outer = lax.ppermute(outer, "gx", [(i, ring(i + (1 if i % 2 else -1))) for i in range(count)])
    inner = lax.ppermute(inner, "gx", [(i, i ^ 1) for i in range(count)])
    sketch_x, raw_y, raw_z, gram = pl.pallas_call(
        first_component_kernel,
        out_shape=[held, held, held, square],
        in_specs=[IN_VMEM] * 3 + [IN_HBM],
        out_specs=[IN_VMEM] * 4,
        scratch_shapes=[pltpu.VMEM((128, 128), jnp.float32), pltpu.SemaphoreType.DMA((3, slabs))],
        compiler_params=limit,
    )(near_vel, near_rim, near_omega, old)
    piece = jax.ShapeDtypeStruct((rank // 4 + 8, rank), jnp.float32)
    sketch_y, sketch_z, keep, send = pl.pallas_call(
        other_components_kernel,
        out_shape=[held, held, piece, piece],
        in_specs=[IN_SMEM] + [IN_VMEM] * 8,
        out_specs=[IN_VMEM] * 4,
        scratch_shapes=[
            pltpu.VMEM((snaps, 2, slabs + 6, rows, cells), jnp.float32),
            pltpu.VMEM((rank, rank), jnp.float32),
            pltpu.VMEM((128, 128), jnp.float32),
        ],
        input_output_aliases={7: 0, 8: 1},
        compiler_params=limit,
    )(parity, near_vel, near_rim, inner, outer, near_omega, gram, raw_y, raw_z)
    swap = lambda k: [(i, i ^ k) for i in range(count)]
    total = keep + lax.ppermute(send, "gx", swap(1))
    step = 2
    while step < count:
        total = total + lax.ppermute(total, "gx", swap(step))
        step *= 2
    other = lax.ppermute(total, "gx", swap(1))
    entries = 3 * slabs * rows * cells * count
    factor, basis = pl.pallas_call(
        functools.partial(basis_kernel, 1.0 / entries),
        out_shape=[square, jax.ShapeDtypeStruct((3, *block), jnp.bfloat16)],
        in_specs=[IN_SMEM] + [IN_VMEM] * 5,
        out_specs=[IN_HBM, IN_HBM],
        scratch_shapes=[
            pltpu.VMEM((rank, rank), jnp.float32),
            pltpu.VMEM((rank, rank), jnp.float32),
            pltpu.VMEM((rank, rank), jnp.float32),
            pltpu.VMEM((WIDE, 128), jnp.float32),
            pltpu.VMEM((3, *block[:-1], rank // 2), jnp.bfloat16),
            pltpu.VMEM((3, *block[:-1], rank // 2), jnp.bfloat16),
            pltpu.SemaphoreType.DMA,
            pltpu.SemaphoreType.DMA((2, 3, slabs)),
        ],
        compiler_params=limit,
    )(parity, total, other, sketch_x, sketch_y, sketch_z)
    return basis, factor


def solution(mesh):
    in_specs = (
        P(None, None, ("rec", "gx"), None, None),
        P(None, None, ("rec", "gx"), None, None),
        P(None, ("rec", "gx"), None, None, None),
        P(),
    )
    out_specs = (P(None, ("rec", "gx"), None, None, None), P("rec", None))
    return jax.shard_map(local, mesh=mesh, in_specs=in_specs, out_specs=out_specs, check_vma=False)
```

```python
import functools

import jax
import jax.numpy as jnp
from jax import lax
from jax.experimental import pallas as pl
from jax.experimental.pallas import tpu as pltpu
from jax.sharding import PartitionSpec as P

COEFS = (0.75, -0.15, 1.0 / 60.0)
IN_SMEM = pl.BlockSpec(memory_space=pltpu.SMEM)
IN_VMEM = pl.BlockSpec(memory_space=pltpu.VMEM)
IN_HBM = pl.BlockSpec(memory_space=pltpu.HBM)
WIDE = 64


def parts_of(x):
    high = x.astype(jnp.bfloat16).astype(jnp.float32)
    rest = x - high
    mid = rest.astype(jnp.bfloat16).astype(jnp.float32)
    return high, mid, rest - mid


def eliminate_below(t_ref, upper, solved, stop):
    order = t_ref.shape[0]
    col = lax.broadcasted_iota(jnp.int32, upper.shape, 1)
    v, w, y = parts_of(jnp.where(col < stop, solved, upper))
    right = jnp.concatenate([v, w, v, y, v, w], axis=0).astype(jnp.bfloat16)
    for base in range(stop // 128 * 128, order, 128):
        a, b, c = parts_of(upper[:, base : base + 128])
        left = jnp.concatenate([a, a, b, a, c, b], axis=0).astype(jnp.bfloat16)
        product = lax.dot_general(left, right, (((0,), (0,)), ((), ())), preferred_element_type=jnp.float32)
        for top in range(max(base, stop), base + 128, WIDE):
            kept = jnp.where((col >= stop - WIDE) & (col < stop), 0.0, t_ref[top : top + WIDE])
            t_ref[top : top + WIDE] = kept - product[top - base : top - base + WIDE]


def factor_block(w_ref, off, spare):
    full = (8, 128)
    sub = lax.broadcasted_iota(jnp.int32, full, 0)
    for j0 in range(0, WIDE, 8):
        c0 = off + j0
        rows = [w_ref[pl.ds(j0 + i, 8, stride=0), :] for i in range(8)]
        a = {}
        for i in range(8):
            for j in range(i, 8):
                a[i, j] = jnp.broadcast_to(rows[i][:, c0 + j : c0 + j + 1], full)
        left, scaled, final = {}, {}, {}
        for k in range(0, 8, 2):
            n = k + 1
            top, mid, low = a[k, k], a[k, n], a[n, n]
            rdet = 1.0 / (top * low - mid * mid)
            p = {i: low * a[k, i] - mid * a[n, i] for i in range(k + 2, 8)}
            q = {i: top * a[n, i] - mid * a[k, i] for i in range(k + 2, 8)}
            for i in range(k + 2, 8):
                for j in range(i, 8):
                    a[i, j] = a[i, j] - (p[i] * a[k, j] + q[i] * a[n, j]) * rdet
                left[k, i], left[n, i] = p[i] * rdet, q[i] * rdet
                rows[i] = rows[i] - (left[k, i] * rows[k] + left[n, i] * rows[n])
            scaled[k] = (low * rows[k] - mid * rows[n]) * rdet
            scaled[n] = (top * rows[n] - mid * rows[k]) * rdet
            root = lax.rsqrt(top)
            ratio = mid * root * root
            final[k] = rows[k] * root
            final[n] = (rows[n] - ratio * rows[k]) * lax.rsqrt(low - mid * ratio)
        for k in reversed(range(8)):
            for i in reversed(range(k // 2 * 2 + 2, 8)):
                scaled[k] = scaled[k] - left[k, i] * scaled[i]
        for q in range(j0 + 8, WIDE, 8):
            old = w_ref[q : q + 8]
            rest = old
            for k in reversed(range(8)):
                rest = rest - jnp.broadcast_to(old[:, c0 + k : c0 + k + 1], full) * scaled[k]
            w_ref[q : q + 8] = rest
        out = final[0]
        for k in range(1, 8):
            out = jnp.where(sub == k, final[k], out)
        w_ref[j0 : j0 + 8] = out
        if spare:
            spare.pop(0)()


def factor_invert(t_ref, u_ref, x_ref, w_ref, spare):
    order = t_ref.shape[0]
    lane = lax.broadcasted_iota(jnp.int32, (WIDE, 128), 1)
    sub = lax.broadcasted_iota(jnp.int32, (WIDE, 128), 0)
    for b0 in range(0, order, WIDE):
        stop = b0 + WIDE
        half, off = b0 // 128, b0 % 128
        inside = (lane >= off) & (lane < off + WIDE)
        here = slice(128 * half, 128 * half + 128)
        w_ref[...] = jnp.where(inside, t_ref[b0:stop, here], jnp.where(lane == sub + (WIDE - off), 1.0, 0.0))
        factor_block(w_ref, off, spare if b0 >= order // 2 else [])
        done = w_ref[...]
        moved = pltpu.roll(done, 64, 1)
        low, high = (moved, done) if off == 0 else (done, moved)
        x1, x2, x3 = parts_of(low)
        y1, y2, _ = parts_of(high)
        r1, r2, r3 = parts_of(t_ref[b0:stop])
        pair = lambda p, q: jnp.where(lane < WIDE, p, q)
        first = jnp.concatenate([pair(x1, y1), pair(x2, y1), pair(x3, y2)], axis=1).astype(jnp.bfloat16)
        second = jnp.concatenate([r1, r2, r1, r3, r1, r2], axis=0).astype(jnp.bfloat16)
        rows = jnp.dot(first, second, preferred_element_type=jnp.float32)
        upper, solved = [], []
        for h in range(order // 128):
            wide = rows[:, 128 * h : 128 * h + 128]
            zero = jnp.zeros_like(wide)
            if h == half:
                upper.append(jnp.where(inside, jnp.where(lane - off >= sub, done, 0.0), jnp.where(lane >= off + WIDE, wide, 0.0)))
                solved.append(jnp.where(inside, moved, jnp.where(lane < off, wide, 0.0)))
            else:
                upper.append(wide if h > half else zero)
                solved.append(wide if h < half else zero)
        upper, solved = jnp.concatenate(upper, axis=1), jnp.concatenate(solved, axis=1)
        u_ref[b0:stop] = upper
        x_ref[b0:stop] = solved
        if stop < order:
            eliminate_below(t_ref, upper, solved, stop)


def wall_diff(plane, count):
    total = jnp.zeros((count, plane.shape[1]), jnp.float32)
    for k, weight in zip((1, 2, 3), COEFS):
        total = total + weight * (plane[3 + k : 3 + k + count] - plane[3 - k : 3 - k + count])
    return total


def span_diff(band, edges):
    past, before = edges
    cells = band.shape[1]
    lane = lax.broadcasted_iota(jnp.int32, band.shape, 1)
    total = jnp.zeros(band.shape, jnp.float32)
    for k, weight in zip((1, 2, 3), COEFS):
        ahead = pltpu.roll(jnp.where(lane < k, past, band), cells - k, 1)
        behind = pltpu.roll(jnp.where(lane >= cells - k, before, band), k, 1)
        total = total + weight * (ahead - behind)
    return total


def stream_diff(planes, at):
    total = jnp.zeros(planes[0].shape, jnp.float32)
    for k, weight in zip((1, 2, 3), COEFS):
        total = total + weight * (planes[at + k] - planes[at - k])
    return total


def span_edges(rim_ref, which, turn_ref):
    snaps, slabs, _, _, rows = rim_ref.shape
    groups = [(s, i) for s in range(snaps) for i in range(slabs)]
    room = turn_ref.shape[0]
    edges = {}
    for start in range(0, len(groups), room // 8):
        some = groups[start : start + room // 8]
        turn_ref[...] = jnp.zeros_like(turn_ref)
        for g, (s, i) in enumerate(some):
            for at, entry in enumerate((3, 4, 5, None, None, 0, 1, 2)):
                if entry is not None:
                    turn_ref[8 * g + at : 8 * g + at + 1, :rows] = rim_ref[s, i, entry, which : which + 1, :]
        turned = turn_ref[...].T[:rows]
        for g, key in enumerate(some):
            edges[key] = (
                pltpu.roll(turned, (room - 8 * g) % room, 1),
                pltpu.roll(turned, (room - 8 - 8 * g) % room, 1),
            )
    return edges


def gain_matrix(omega, rows):
    snaps, rank = omega.shape
    high = omega.astype(jnp.bfloat16).astype(jnp.float32)
    low = omega - high
    pieces = [jnp.broadcast_to(part[s : s + 1], (rows, rank)) for part in (high, high, low) for s in range(snaps)]
    depth = 3 * snaps * rows
    pieces.append(jnp.zeros((-depth % 128, rank), jnp.float32))
    return jnp.concatenate(pieces, axis=0).astype(jnp.bfloat16)


def update_block(vort, right, new_ref, acc_ref):
    rows, cells, rank = new_ref.shape
    high = [v.astype(jnp.bfloat16).astype(jnp.float32) for v in vort]
    low = [v - h for v, h in zip(vort, high)]
    depth = right.shape[0]
    rest = jnp.zeros((depth - 3 * rows * len(vort), cells), jnp.float32)
    turned = jnp.concatenate(high + low + high + [rest], axis=0).T.astype(jnp.bfloat16)
    lane = lax.broadcasted_iota(jnp.int32, (1, depth), 1)
    for y in range(rows):
        mask = jnp.where(lax.rem(lane, rows) == y, 1.0, 0.0).astype(jnp.bfloat16)
        gain = jnp.dot(turned * mask, right, preferred_element_type=jnp.float32)
        new_ref[y] = (new_ref[y].astype(jnp.float32) + gain).astype(jnp.bfloat16)
    block = new_ref[...].reshape(rows * cells, rank)
    acc_ref[...] += lax.dot_general(block, block, (((0,), (0,)), ((), ())), preferred_element_type=jnp.float32)


def start_kernel(vel_in, rim_in, omega_in, band_ref, vel_ref, rim_ref, omega_ref, sems):
    snaps, _, slabs, height, _ = vel_ref.shape
    rows = height - 6
    copies = [
        pltpu.make_async_copy(source, target, sems.at[n])
        for n, (source, target) in enumerate(((vel_in, vel_ref), (rim_in, rim_ref), (omega_in, omega_ref)))
    ]
    for copy in copies:
        copy.start()
    copies[0].wait()
    for s in range(snaps):
        for c in range(2):
            for i in range(slabs):
                at = ((s * 2 + c) * slabs + i) * rows
                band_ref[at : at + rows] = vel_ref[s, 1 + c, i, 3 : 3 + rows]
    for copy in copies[1:]:
        copy.wait()


def first_component_kernel(
    vel_ref, rim_ref, omega_ref, old_ref,
    x_ref, y_ref, z_ref, gram_ref, right_ref, part_ref, turn_ref, sems,
):
    snaps, _, slabs, height, _ = vel_ref.shape
    rows = height - 6
    copies = [
        pltpu.make_async_copy(old_ref.at[c, i], new_ref.at[i], sems.at[c, i])
        for c, new_ref in enumerate((x_ref, y_ref, z_ref))
        for i in range(slabs)
    ]
    for copy in copies:
        copy.start()
    gram_ref[...] = jnp.zeros_like(gram_ref)
    right = gain_matrix(omega_ref[...], rows)
    right_ref[...] = right
    edges = span_edges(rim_ref, 1, turn_ref)
    for i in range(slabs):
        vort = [
            wall_diff(vel_ref[s, 2, i], rows) - span_diff(vel_ref[s, 1, i, 3 : 3 + rows], edges[s, i])
            for s in range(snaps)
        ]
        copies[i].wait()
        update_block(vort, right, x_ref.at[i], gram_ref)
    edges = span_edges(rim_ref, 0, turn_ref)
    for s in range(snaps):
        for i in range(slabs):
            part_ref[0, s, i] = span_diff(vel_ref[s, 0, i, 3 : 3 + rows], edges[s, i])
            part_ref[1, s, i] = wall_diff(vel_ref[s, 0, i], rows)
    for copy in copies[slabs:]:
        copy.wait()


def pack(gram_ref, first, keep_ref, send_ref):
    half = gram_ref.shape[0] // 2
    row = lax.broadcasted_iota(jnp.int32, (half, half), 0)
    col = lax.broadcasted_iota(jnp.int32, (half, half), 1)
    low = gram_ref[half:, half:]
    mixed = jnp.where(row <= col, gram_ref[:half, :half], low)
    diag = jnp.sum(jnp.where(row == col, low, 0.0), axis=0, keepdims=True)
    packed = jnp.concatenate([gram_ref[:half, half:], mixed], axis=1)
    part = half // 2
    extra = jnp.broadcast_to(jnp.concatenate([diag, diag], axis=1), (8, 2 * half))
    upper, lower = packed[:part], packed[part:]
    keep_ref[:part] = jnp.where(first, upper, lower)
    send_ref[:part] = jnp.where(first, lower, upper)
    keep_ref[part:] = extra
    send_ref[part:] = extra


def other_components_kernel(
    parity_ref, vel_ref, part_ref, inner_ref, outer_ref, right_ref, start_ref, old_y_ref, old_z_ref,
    y_ref, z_ref, keep_ref, send_ref, wide_ref, gram_ref,
):
    del old_y_ref, old_z_ref
    snaps, _, slabs, height, _ = vel_ref.shape
    rows = height - 6
    gram_ref[...] = start_ref[...]
    right = right_ref[...]
    even = parity_ref[0] == 0
    for s in range(snaps):
        for c in range(2):
            for k in range(3):
                at = ((s * 2 + c) * 3 + k) * rows
                inner, outer = inner_ref[at : at + rows], outer_ref[at : at + rows]
                wide_ref[s, c, k] = jnp.where(even, outer, inner)
                wide_ref[s, c, 3 + slabs + k] = jnp.where(even, inner, outer)
            for i in range(slabs):
                wide_ref[s, c, 3 + i] = vel_ref[s, 1 + c, i, 3 : 3 + rows]
    for i in range(slabs):
        for c, new_ref in enumerate((y_ref, z_ref)):
            vort = []
            for s in range(snaps):
                along = stream_diff([wide_ref[s, 1 - c, i + k] for k in range(7)], 3)
                if c == 0:
                    vort.append(part_ref[0, s, i] - along)
                else:
                    vort.append(along - part_ref[1, s, i])
            update_block(vort, right, new_ref.at[i], gram_ref)
    pack(gram_ref, even, keep_ref, send_ref)


def unpack(packed, part_diag, work_ref):
    half = packed.shape[0]
    cross, mixed = packed[:, :half], packed[:, half:]
    row = lax.broadcasted_iota(jnp.int32, (half, half), 0)
    col = lax.broadcasted_iota(jnp.int32, (half, half), 1)
    turned = mixed.T
    diag = jnp.broadcast_to(part_diag[:, :half], (half, half))
    work_ref[:half, :half] = jnp.where(row <= col, mixed, turned)
    work_ref[:half, half:] = cross
    work_ref[half:, :half] = cross.T
    work_ref[half:, half:] = jnp.where(row > col, mixed, jnp.where(row < col, turned, diag))


def basis_kernel(
    scale, parity_ref, mine_ref, other_ref, x_ref, y_ref, z_ref, factor_ref, basis_ref,
    work_ref, upper_ref, solved_ref, block_ref, low_ref, high_ref, factor_sem, sems,
):
    order = work_ref.shape[0]
    part = order // 4
    first = parity_ref[0] == 0
    mine, other = mine_ref[...] * scale, other_ref[...] * scale
    top, bottom = jnp.where(first, mine[:part], other[:part]), jnp.where(first, other[:part], mine[:part])
    unpack(jnp.concatenate([top, bottom], axis=0), mine[part : part + 1], work_ref)
    half = order // 2
    blocks = [(c, i, ref) for c, ref in enumerate((x_ref, y_ref, z_ref)) for i in range(ref.shape[0])]
    copies = []

    def multiply(c, i, sketch_ref, stage_ref, side, get_inverse):
        _, rows, cells, _ = sketch_ref.shape
        depth = half * (side + 1)
        step = 2 - rows % 2
        for y in range(0, rows, step):
            block = sketch_ref[i, y : y + step, :, :depth].reshape(step * cells, depth)
            product = jnp.dot(block, get_inverse(), preferred_element_type=jnp.float32)
            stage_ref[c, i, y : y + step] = product.astype(jnp.bfloat16).reshape(step, cells, half)
        columns = pl.ds(half * side, half)
        copy = pltpu.make_async_copy(
            stage_ref.at[c, i], basis_ref.at[c, i, :, :, columns], sems.at[side, c, i]
        )
        copy.start()
        copies.append(copy)

    made = []

    def first_inverse():
        if not made:
            made.append(solved_ref[:half, :half].T.astype(jnp.bfloat16))
        return made[0]

    spare = [functools.partial(multiply, *block, low_ref, 0, first_inverse) for block in blocks]
    factor_invert(work_ref, upper_ref, solved_ref, block_ref, spare)
    for piece in spare:
        piece()
    factor_copy = pltpu.make_async_copy(upper_ref, factor_ref, factor_sem)
    factor_copy.start()
    inverse = solved_ref[half:].T.astype(jnp.bfloat16)
    for block in blocks:
        multiply(*block, high_ref, 1, lambda: inverse)
    for copy in [factor_copy] + copies:
        copy.wait()


def local(velocity, span_rim, sketch_old, omega):
    snaps, _, slabs, height, cells = velocity.shape
    rows = height - 6
    rank = omega.shape[1]
    count = lax.axis_size("gx")
    limit = pltpu.CompilerParams(vmem_limit_bytes=24 << 20)
    place = lax.axis_index("gx")
    parity = (place % 2).reshape(1)
    rim = span_rim.transpose(0, 2, 4, 1, 3)
    block = (slabs, rows, cells, rank)
    square = jax.ShapeDtypeStruct((rank, rank), jnp.float32)
    held = pltpu.VMEM(block, jnp.bfloat16)
    old = pltpu.with_memory_space_constraint(sketch_old, pltpu.HBM)
    small = [pltpu.with_memory_space_constraint(x, pltpu.HBM) for x in (velocity, rim, omega)]
    planes, near_vel, near_rim, near_omega = pl.pallas_call(
        start_kernel,
        out_shape=[pltpu.VMEM((snaps * 2 * slabs * rows, cells), jnp.float32)]
        + [pltpu.VMEM(x.shape, x.dtype) for x in (velocity, rim, omega)],
        in_specs=[IN_HBM] * 3,
        out_specs=[IN_VMEM] * 4,
        scratch_shapes=[pltpu.SemaphoreType.DMA((3,))],
        compiler_params=limit,
    )(*small)
    inner, outer = planes, planes
    if slabs > 3:
        whole = planes.reshape(snaps * 2, slabs, rows, cells)
        head, tail = (x.reshape(-1, cells) for x in (whole[:, :3], whole[:, slabs - 3 :]))
        even = place % 2 == 0
        inner, outer = jnp.where(even, tail, head), jnp.where(even, head, tail)
    ring = lambda i: i % count
    outer = lax.ppermute(outer, "gx", [(i, ring(i + (1 if i % 2 else -1))) for i in range(count)])
    inner = lax.ppermute(inner, "gx", [(i, i ^ 1) for i in range(count)])
    depth = 3 * snaps * rows
    sketch_x, raw_y, raw_z, gram, right, partial = pl.pallas_call(
        first_component_kernel,
        out_shape=[held, held, held, square]
        + [pltpu.VMEM((depth + -depth % 128, rank), jnp.bfloat16)]
        + [pltpu.VMEM((2, snaps, slabs, rows, cells), jnp.float32)],
        in_specs=[IN_VMEM] * 3 + [IN_HBM],
        out_specs=[IN_VMEM] * 6,
        scratch_shapes=[pltpu.VMEM((128, 128), jnp.float32), pltpu.SemaphoreType.DMA((3, slabs))],
        compiler_params=limit,
    )(near_vel, near_rim, near_omega, old)
    piece = jax.ShapeDtypeStruct((rank // 4 + 8, rank), jnp.float32)
    sketch_y, sketch_z, keep, send = pl.pallas_call(
        other_components_kernel,
        out_shape=[held, held, piece, piece],
        in_specs=[IN_SMEM] + [IN_VMEM] * 8,
        out_specs=[IN_VMEM] * 4,
        scratch_shapes=[
            pltpu.VMEM((snaps, 2, slabs + 6, rows, cells), jnp.float32),
            pltpu.VMEM((rank, rank), jnp.float32),
        ],
        input_output_aliases={7: 0, 8: 1},
        compiler_params=limit,
    )(parity, near_vel, partial, inner, outer, right, gram, raw_y, raw_z)
    swap = lambda k: [(i, i ^ k) for i in range(count)]
    total = keep + lax.ppermute(send, "gx", swap(1))
    step = 2
    while step < count:
        total = total + lax.ppermute(total, "gx", swap(step))
        step *= 2
    other = lax.ppermute(total, "gx", swap(1))
    entries = 3 * slabs * rows * cells * count
    factor, basis = pl.pallas_call(
        functools.partial(basis_kernel, 1.0 / entries),
        out_shape=[square, jax.ShapeDtypeStruct((3, *block), jnp.bfloat16)],
        in_specs=[IN_SMEM] + [IN_VMEM] * 5,
        out_specs=[IN_HBM, IN_HBM],
        scratch_shapes=[
            pltpu.VMEM((rank, rank), jnp.float32),
            pltpu.VMEM((rank, rank), jnp.float32),
            pltpu.VMEM((rank, rank), jnp.float32),
            pltpu.VMEM((WIDE, 128), jnp.float32),
            pltpu.VMEM((3, *block[:-1], rank // 2), jnp.bfloat16),
            pltpu.VMEM((3, *block[:-1], rank // 2), jnp.bfloat16),
            pltpu.SemaphoreType.DMA,
            pltpu.SemaphoreType.DMA((2, 3, slabs)),
        ],
        compiler_params=limit,
    )(parity, total, other, sketch_x, sketch_y, sketch_z)
    return basis, factor


def solution(mesh):
    in_specs = (
        P(None, None, ("rec", "gx"), None, None),
        P(None, None, ("rec", "gx"), None, None),
        P(None, ("rec", "gx"), None, None, None),
        P(),
    )
    out_specs = (P(None, ("rec", "gx"), None, None, None), P("rec", None))
    return jax.shard_map(local, mesh=mesh, in_specs=in_specs, out_specs=out_specs, check_vma=False)
```

```python
import functools

import jax
import jax.numpy as jnp
from jax import lax
from jax.experimental import pallas as pl
from jax.experimental.pallas import tpu as pltpu
from jax.sharding import PartitionSpec as P

COEFS = (0.75, -0.15, 1.0 / 60.0)
IN_SMEM = pl.BlockSpec(memory_space=pltpu.SMEM)
IN_VMEM = pl.BlockSpec(memory_space=pltpu.VMEM)
IN_HBM = pl.BlockSpec(memory_space=pltpu.HBM)
WIDE = 64


def parts_of(x):
    high = x.astype(jnp.bfloat16).astype(jnp.float32)
    rest = x - high
    mid = rest.astype(jnp.bfloat16).astype(jnp.float32)
    return high, mid, rest - mid


def eliminate_below(t_ref, upper, solved, stop):
    order = t_ref.shape[0]
    col = lax.broadcasted_iota(jnp.int32, upper.shape, 1)
    v, w, y = parts_of(jnp.where(col < stop, solved, upper))
    right = jnp.concatenate([v, w, v, y, v, w], axis=0).astype(jnp.bfloat16)
    for base in range(stop // 128 * 128, order, 128):
        a, b, c = parts_of(upper[:, base : base + 128])
        left = jnp.concatenate([a, a, b, a, c, b], axis=0).astype(jnp.bfloat16)
        product = lax.dot_general(left, right, (((0,), (0,)), ((), ())), preferred_element_type=jnp.float32)
        for top in range(max(base, stop), base + 128, WIDE):
            kept = jnp.where((col >= stop - WIDE) & (col < stop), 0.0, t_ref[top : top + WIDE])
            t_ref[top : top + WIDE] = kept - product[top - base : top - base + WIDE]


def factor_block(w_ref, off, spare):
    full = (8, 128)
    sub = lax.broadcasted_iota(jnp.int32, full, 0)
    for j0 in range(0, WIDE, 8):
        c0 = off + j0
        rows = [w_ref[pl.ds(j0 + i, 8, stride=0), :] for i in range(8)]
        a = {}
        for i in range(8):
            for j in range(i, 8):
                a[i, j] = jnp.broadcast_to(rows[i][:, c0 + j : c0 + j + 1], full)
        left, scaled, final = {}, {}, {}
        for k in range(0, 8, 2):
            n = k + 1
            top, mid, low = a[k, k], a[k, n], a[n, n]
            rdet = 1.0 / (top * low - mid * mid)
            p = {i: low * a[k, i] - mid * a[n, i] for i in range(k + 2, 8)}
            q = {i: top * a[n, i] - mid * a[k, i] for i in range(k + 2, 8)}
            for i in range(k + 2, 8):
                for j in range(i, 8):
                    a[i, j] = a[i, j] - (p[i] * a[k, j] + q[i] * a[n, j]) * rdet
                left[k, i], left[n, i] = p[i] * rdet, q[i] * rdet
                rows[i] = rows[i] - (left[k, i] * rows[k] + left[n, i] * rows[n])
            scaled[k] = (low * rows[k] - mid * rows[n]) * rdet
            scaled[n] = (top * rows[n] - mid * rows[k]) * rdet
            root = lax.rsqrt(top)
            ratio = mid * root * root
            final[k] = rows[k] * root
            final[n] = (rows[n] - ratio * rows[k]) * lax.rsqrt(low - mid * ratio)
        for k in reversed(range(8)):
            for i in reversed(range(k // 2 * 2 + 2, 8)):
                scaled[k] = scaled[k] - left[k, i] * scaled[i]
        for q in range(j0 + 8, WIDE, 8):
            old = w_ref[q : q + 8]
            rest = old
            for k in reversed(range(8)):
                rest = rest - jnp.broadcast_to(old[:, c0 + k : c0 + k + 1], full) * scaled[k]
            w_ref[q : q + 8] = rest
        out = final[0]
        for k in range(1, 8):
            out = jnp.where(sub == k, final[k], out)
        w_ref[j0 : j0 + 8] = out
        if spare:
            spare.pop(0)()


def factor_invert(t_ref, u_ref, x_ref, w_ref, spare):
    order = t_ref.shape[0]
    lane = lax.broadcasted_iota(jnp.int32, (WIDE, 128), 1)
    sub = lax.broadcasted_iota(jnp.int32, (WIDE, 128), 0)
    for b0 in range(0, order, WIDE):
        stop = b0 + WIDE
        half, off = b0 // 128, b0 % 128
        inside = (lane >= off) & (lane < off + WIDE)
        here = slice(128 * half, 128 * half + 128)
        w_ref[...] = jnp.where(inside, t_ref[b0:stop, here], jnp.where(lane == sub + (WIDE - off), 1.0, 0.0))
        factor_block(w_ref, off, spare if b0 >= order // 2 else [])
        done = w_ref[...]
        moved = pltpu.roll(done, 64, 1)
        low, high = (moved, done) if off == 0 else (done, moved)
        x1, x2, x3 = parts_of(low)
        y1, y2, _ = parts_of(high)
        r1, r2, r3 = parts_of(t_ref[b0:stop])
        pair = lambda p, q: jnp.where(lane < WIDE, p, q)
        first = jnp.concatenate([pair(x1, y1), pair(x2, y1), pair(x3, y2)], axis=1).astype(jnp.bfloat16)
        second = jnp.concatenate([r1, r2, r1, r3, r1, r2], axis=0).astype(jnp.bfloat16)
        rows = jnp.dot(first, second, preferred_element_type=jnp.float32)
        upper, solved = [], []
        for h in range(order // 128):
            wide = rows[:, 128 * h : 128 * h + 128]
            zero = jnp.zeros_like(wide)
            if h == half:
                upper.append(jnp.where(inside, jnp.where(lane - off >= sub, done, 0.0), jnp.where(lane >= off + WIDE, wide, 0.0)))
                solved.append(jnp.where(inside, moved, jnp.where(lane < off, wide, 0.0)))
            else:
                upper.append(wide if h > half else zero)
                solved.append(wide if h < half else zero)
        upper, solved = jnp.concatenate(upper, axis=1), jnp.concatenate(solved, axis=1)
        u_ref[b0:stop] = upper
        x_ref[b0:stop] = solved
        if stop < order:
            eliminate_below(t_ref, upper, solved, stop)


def wall_diff(plane, count):
    total = jnp.zeros((count, plane.shape[1]), jnp.float32)
    for k, weight in zip((1, 2, 3), COEFS):
        total = total + weight * (plane[3 + k : 3 + k + count] - plane[3 - k : 3 - k + count])
    return total


def span_diff(band, edges):
    past, before = edges
    cells = band.shape[1]
    lane = lax.broadcasted_iota(jnp.int32, band.shape, 1)
    total = jnp.zeros(band.shape, jnp.float32)
    for k, weight in zip((1, 2, 3), COEFS):
        ahead = pltpu.roll(jnp.where(lane < k, past, band), cells - k, 1)
        behind = pltpu.roll(jnp.where(lane >= cells - k, before, band), k, 1)
        total = total + weight * (ahead - behind)
    return total


def stream_diff(planes, at):
    total = jnp.zeros(planes[0].shape, jnp.float32)
    for k, weight in zip((1, 2, 3), COEFS):
        total = total + weight * (planes[at + k] - planes[at - k])
    return total


def span_edges(rim_ref, which, turn_ref):
    snaps, slabs, _, _, rows = rim_ref.shape
    groups = [(s, i) for s in range(snaps) for i in range(slabs)]
    room = turn_ref.shape[0]
    edges = {}
    for start in range(0, len(groups), room // 8):
        some = groups[start : start + room // 8]
        turn_ref[...] = jnp.zeros_like(turn_ref)
        for g, (s, i) in enumerate(some):
            for at, entry in enumerate((3, 4, 5, None, None, 0, 1, 2)):
                if entry is not None:
                    turn_ref[8 * g + at : 8 * g + at + 1, :rows] = rim_ref[s, i, entry, which : which + 1, :]
        turned = turn_ref[...].T[:rows]
        for g, key in enumerate(some):
            edges[key] = (
                pltpu.roll(turned, (room - 8 * g) % room, 1),
                pltpu.roll(turned, (room - 8 - 8 * g) % room, 1),
            )
    return edges


def gain_matrix(omega, rows):
    snaps, rank = omega.shape
    high = omega.astype(jnp.bfloat16).astype(jnp.float32)
    low = omega - high
    pieces = [jnp.broadcast_to(part[s : s + 1], (rows, rank)) for part in (high, high, low) for s in range(snaps)]
    depth = 3 * snaps * rows
    pieces.append(jnp.zeros((-depth % 128, rank), jnp.float32))
    return jnp.concatenate(pieces, axis=0).astype(jnp.bfloat16)


def update_block(vort, right, new_ref, acc_ref):
    rows, cells, rank = new_ref.shape
    high = [v.astype(jnp.bfloat16).astype(jnp.float32) for v in vort]
    low = [v - h for v, h in zip(vort, high)]
    depth = right.shape[0]
    rest = jnp.zeros((depth - 3 * rows * len(vort), cells), jnp.float32)
    turned = jnp.concatenate(high + low + high + [rest], axis=0).T.astype(jnp.bfloat16)
    lane = lax.broadcasted_iota(jnp.int32, (1, depth), 1)
    for y in range(rows):
        mask = jnp.where(lax.rem(lane, rows) == y, 1.0, 0.0).astype(jnp.bfloat16)
        gain = jnp.dot(turned * mask, right, preferred_element_type=jnp.float32)
        new_ref[y] = (new_ref[y].astype(jnp.float32) + gain).astype(jnp.bfloat16)
    block = new_ref[...].reshape(rows * cells, rank)
    acc_ref[...] += lax.dot_general(block, block, (((0,), (0,)), ((), ())), preferred_element_type=jnp.float32)


def start_kernel(vel_in, rim_in, omega_in, band_ref, vel_ref, rim_ref, omega_ref, sems):
    snaps, _, slabs, height, _ = vel_ref.shape
    rows = height - 6
    copies = [
        pltpu.make_async_copy(source, target, sems.at[n])
        for n, (source, target) in enumerate(((vel_in, vel_ref), (rim_in, rim_ref), (omega_in, omega_ref)))
    ]
    for copy in copies:
        copy.start()
    copies[0].wait()
    for s in range(snaps):
        for c in range(2):
            for i in range(slabs):
                at = ((s * 2 + c) * slabs + i) * rows
                band_ref[at : at + rows] = vel_ref[s, 1 + c, i, 3 : 3 + rows]
    for copy in copies[1:]:
        copy.wait()


def first_component_kernel(
    vel_ref, rim_ref, omega_ref, old_ref,
    x_ref, y_ref, z_ref, gram_ref, right_ref, part_ref, turn_ref, sems,
):
    snaps, _, slabs, height, _ = vel_ref.shape
    rows = height - 6
    copies = [
        pltpu.make_async_copy(old_ref.at[c, i], new_ref.at[i], sems.at[c, i])
        for c, new_ref in enumerate((x_ref, y_ref, z_ref))
        for i in range(slabs)
    ]
    for copy in copies:
        copy.start()
    gram_ref[...] = jnp.zeros_like(gram_ref)
    right = gain_matrix(omega_ref[...], rows)
    right_ref[...] = right
    edges = span_edges(rim_ref, 0, turn_ref)
    for s in range(snaps):
        for i in range(slabs):
            part_ref[0, s, i] = span_diff(vel_ref[s, 0, i, 3 : 3 + rows], edges[s, i])
            part_ref[1, s, i] = wall_diff(vel_ref[s, 0, i], rows)
    edges = span_edges(rim_ref, 1, turn_ref)
    for i in range(slabs):
        vort = [
            wall_diff(vel_ref[s, 2, i], rows) - span_diff(vel_ref[s, 1, i, 3 : 3 + rows], edges[s, i])
            for s in range(snaps)
        ]
        copies[i].wait()
        update_block(vort, right, x_ref.at[i], gram_ref)
    for copy in copies[slabs:]:
        copy.wait()


def pack(gram_ref, first, keep_ref, send_ref):
    half = gram_ref.shape[0] // 2
    row = lax.broadcasted_iota(jnp.int32, (half, half), 0)
    col = lax.broadcasted_iota(jnp.int32, (half, half), 1)
    low = gram_ref[half:, half:]
    mixed = jnp.where(row <= col, gram_ref[:half, :half], low)
    diag = jnp.sum(jnp.where(row == col, low, 0.0), axis=0, keepdims=True)
    packed = jnp.concatenate([gram_ref[:half, half:], mixed], axis=1)
    part = half // 2
    extra = jnp.broadcast_to(jnp.concatenate([diag, diag], axis=1), (8, 2 * half))
    upper, lower = packed[:part], packed[part:]
    keep_ref[:part] = jnp.where(first, upper, lower)
    send_ref[:part] = jnp.where(first, lower, upper)
    keep_ref[part:] = extra
    send_ref[part:] = extra


def other_components_kernel(
    parity_ref, vel_ref, part_ref, inner_ref, outer_ref, right_ref, start_ref, old_y_ref, old_z_ref,
    y_ref, z_ref, keep_ref, send_ref, wide_ref, gram_ref,
):
    del old_y_ref, old_z_ref
    snaps, _, slabs, height, _ = vel_ref.shape
    rows = height - 6
    gram_ref[...] = start_ref[...]
    right = right_ref[...]
    even = parity_ref[0] == 0
    for s in range(snaps):
        for c in range(2):
            for k in range(3):
                at = ((s * 2 + c) * 3 + k) * rows
                inner, outer = inner_ref[at : at + rows], outer_ref[at : at + rows]
                wide_ref[s, c, k] = jnp.where(even, outer, inner)
                wide_ref[s, c, 3 + slabs + k] = jnp.where(even, inner, outer)
            for i in range(slabs):
                wide_ref[s, c, 3 + i] = vel_ref[s, 1 + c, i, 3 : 3 + rows]
    for i in range(slabs):
        for c, new_ref in enumerate((y_ref, z_ref)):
            vort = []
            for s in range(snaps):
                along = stream_diff([wide_ref[s, 1 - c, i + k] for k in range(7)], 3)
                if c == 0:
                    vort.append(part_ref[0, s, i] - along)
                else:
                    vort.append(along - part_ref[1, s, i])
            update_block(vort, right, new_ref.at[i], gram_ref)
    pack(gram_ref, even, keep_ref, send_ref)


def unpack(packed, part_diag, work_ref):
    half = packed.shape[0]
    cross, mixed = packed[:, :half], packed[:, half:]
    row = lax.broadcasted_iota(jnp.int32, (half, half), 0)
    col = lax.broadcasted_iota(jnp.int32, (half, half), 1)
    turned = mixed.T
    diag = jnp.broadcast_to(part_diag[:, :half], (half, half))
    work_ref[:half, :half] = jnp.where(row <= col, mixed, turned)
    work_ref[:half, half:] = cross
    work_ref[half:, :half] = cross.T
    work_ref[half:, half:] = jnp.where(row > col, mixed, jnp.where(row < col, turned, diag))


def basis_kernel(
    scale, parity_ref, mine_ref, other_ref, x_ref, y_ref, z_ref, factor_ref, basis_ref,
    work_ref, upper_ref, solved_ref, block_ref, low_ref, high_ref, factor_sem, sems,
):
    order = work_ref.shape[0]
    part = order // 4
    first = parity_ref[0] == 0
    mine, other = mine_ref[...] * scale, other_ref[...] * scale
    top, bottom = jnp.where(first, mine[:part], other[:part]), jnp.where(first, other[:part], mine[:part])
    unpack(jnp.concatenate([top, bottom], axis=0), mine[part : part + 1], work_ref)
    half = order // 2
    blocks = [(c, i, ref) for c, ref in enumerate((x_ref, y_ref, z_ref)) for i in range(ref.shape[0])]
    copies = []

    def multiply(c, i, sketch_ref, stage_ref, side, get_inverse):
        _, rows, cells, _ = sketch_ref.shape
        depth = half * (side + 1)
        step = 2 - rows % 2
        for y in range(0, rows, step):
            block = sketch_ref[i, y : y + step, :, :depth].reshape(step * cells, depth)
            product = jnp.dot(block, get_inverse(), preferred_element_type=jnp.float32)
            stage_ref[c, i, y : y + step] = product.astype(jnp.bfloat16).reshape(step, cells, half)
        columns = pl.ds(half * side, half)
        copy = pltpu.make_async_copy(
            stage_ref.at[c, i], basis_ref.at[c, i, :, :, columns], sems.at[side, c, i]
        )
        copy.start()
        copies.append(copy)

    made = []

    def first_inverse():
        if not made:
            made.append(solved_ref[:half, :half].T.astype(jnp.bfloat16))
        return made[0]

    spare = [functools.partial(multiply, *block, low_ref, 0, first_inverse) for block in blocks]
    factor_invert(work_ref, upper_ref, solved_ref, block_ref, spare)
    for piece in spare:
        piece()
    factor_copy = pltpu.make_async_copy(upper_ref, factor_ref, factor_sem)
    factor_copy.start()
    inverse = solved_ref[half:].T.astype(jnp.bfloat16)
    for block in blocks:
        multiply(*block, high_ref, 1, lambda: inverse)
    for copy in [factor_copy] + copies:
        copy.wait()


def local(velocity, span_rim, sketch_old, omega):
    snaps, _, slabs, height, cells = velocity.shape
    rows = height - 6
    rank = omega.shape[1]
    count = lax.axis_size("gx")
    limit = pltpu.CompilerParams(vmem_limit_bytes=24 << 20)
    place = lax.axis_index("gx")
    parity = (place % 2).reshape(1)
    rim = span_rim.transpose(0, 2, 4, 1, 3)
    block = (slabs, rows, cells, rank)
    square = jax.ShapeDtypeStruct((rank, rank), jnp.float32)
    held = pltpu.VMEM(block, jnp.bfloat16)
    old = pltpu.with_memory_space_constraint(sketch_old, pltpu.HBM)
    small = [pltpu.with_memory_space_constraint(x, pltpu.HBM) for x in (velocity, rim, omega)]
    planes, near_vel, near_rim, near_omega = pl.pallas_call(
        start_kernel,
        out_shape=[pltpu.VMEM((snaps * 2 * slabs * rows, cells), jnp.float32)]
        + [pltpu.VMEM(x.shape, x.dtype) for x in (velocity, rim, omega)],
        in_specs=[IN_HBM] * 3,
        out_specs=[IN_VMEM] * 4,
        scratch_shapes=[pltpu.SemaphoreType.DMA((3,))],
        compiler_params=limit,
    )(*small)
    inner, outer = planes, planes
    if slabs > 3:
        whole = planes.reshape(snaps * 2, slabs, rows, cells)
        head, tail = (x.reshape(-1, cells) for x in (whole[:, :3], whole[:, slabs - 3 :]))
        even = place % 2 == 0
        inner, outer = jnp.where(even, tail, head), jnp.where(even, head, tail)
    ring = lambda i: i % count
    outer = lax.ppermute(outer, "gx", [(i, ring(i + (1 if i % 2 else -1))) for i in range(count)])
    inner = lax.ppermute(inner, "gx", [(i, i ^ 1) for i in range(count)])
    depth = 3 * snaps * rows
    sketch_x, raw_y, raw_z, gram, right, partial = pl.pallas_call(
        first_component_kernel,
        out_shape=[held, held, held, square]
        + [pltpu.VMEM((depth + -depth % 128, rank), jnp.bfloat16)]
        + [pltpu.VMEM((2, snaps, slabs, rows, cells), jnp.float32)],
        in_specs=[IN_VMEM] * 3 + [IN_HBM],
        out_specs=[IN_VMEM] * 6,
        scratch_shapes=[pltpu.VMEM((128, 128), jnp.float32), pltpu.SemaphoreType.DMA((3, slabs))],
        compiler_params=limit,
    )(near_vel, near_rim, near_omega, old)
    piece = jax.ShapeDtypeStruct((rank // 4 + 8, rank), jnp.float32)
    sketch_y, sketch_z, keep, send = pl.pallas_call(
        other_components_kernel,
        out_shape=[held, held, piece, piece],
        in_specs=[IN_SMEM] + [IN_VMEM] * 8,
        out_specs=[IN_VMEM] * 4,
        scratch_shapes=[
            pltpu.VMEM((snaps, 2, slabs + 6, rows, cells), jnp.float32),
            pltpu.VMEM((rank, rank), jnp.float32),
        ],
        input_output_aliases={7: 0, 8: 1},
        compiler_params=limit,
    )(parity, near_vel, partial, inner, outer, right, gram, raw_y, raw_z)
    swap = lambda k: [(i, i ^ k) for i in range(count)]
    total = keep + lax.ppermute(send, "gx", swap(1))
    step = 2
    while step < count:
        total = total + lax.ppermute(total, "gx", swap(step))
        step *= 2
    other = lax.ppermute(total, "gx", swap(1))
    entries = 3 * slabs * rows * cells * count
    factor, basis = pl.pallas_call(
        functools.partial(basis_kernel, 1.0 / entries),
        out_shape=[square, jax.ShapeDtypeStruct((3, *block), jnp.bfloat16)],
        in_specs=[IN_SMEM] + [IN_VMEM] * 5,
        out_specs=[IN_HBM, IN_HBM],
        scratch_shapes=[
            pltpu.VMEM((rank, rank), jnp.float32),
            pltpu.VMEM((rank, rank), jnp.float32),
            pltpu.VMEM((rank, rank), jnp.float32),
            pltpu.VMEM((WIDE, 128), jnp.float32),
            pltpu.VMEM((3, *block[:-1], rank // 2), jnp.bfloat16),
            pltpu.VMEM((3, *block[:-1], rank // 2), jnp.bfloat16),
            pltpu.SemaphoreType.DMA,
            pltpu.SemaphoreType.DMA((2, 3, slabs)),
        ],
        compiler_params=limit,
    )(parity, total, other, sketch_x, sketch_y, sketch_z)
    return basis, factor


def solution(mesh):
    in_specs = (
        P(None, None, ("rec", "gx"), None, None),
        P(None, None, ("rec", "gx"), None, None),
        P(None, ("rec", "gx"), None, None, None),
        P(),
    )
    out_specs = (P(None, ("rec", "gx"), None, None, None), P("rec", None))
    return jax.shard_map(local, mesh=mesh, in_specs=in_specs, out_specs=out_specs, check_vma=False)
```

```python
import functools

import jax
import jax.numpy as jnp
from jax import lax
from jax.experimental import pallas as pl
from jax.experimental.pallas import tpu as pltpu
from jax.sharding import PartitionSpec as P

COEFS = (0.75, -0.15, 1.0 / 60.0)
IN_SMEM = pl.BlockSpec(memory_space=pltpu.SMEM)
IN_VMEM = pl.BlockSpec(memory_space=pltpu.VMEM)
IN_HBM = pl.BlockSpec(memory_space=pltpu.HBM)
WIDE = 64


def parts_of(x):
    high = x.astype(jnp.bfloat16).astype(jnp.float32)
    rest = x - high
    mid = rest.astype(jnp.bfloat16).astype(jnp.float32)
    return high, mid, rest - mid


def eliminate_below(t_ref, upper, solved, stop):
    order = t_ref.shape[0]
    col = lax.broadcasted_iota(jnp.int32, upper.shape, 1)
    v, w, y = parts_of(jnp.where(col < stop, solved, upper))
    right = jnp.concatenate([v, w, v, y, v, w], axis=0).astype(jnp.bfloat16)
    for base in range(stop // 128 * 128, order, 128):
        a, b, c = parts_of(upper[:, base : base + 128])
        left = jnp.concatenate([a, a, b, a, c, b], axis=0).astype(jnp.bfloat16)
        product = lax.dot_general(left, right, (((0,), (0,)), ((), ())), preferred_element_type=jnp.float32)
        for top in range(max(base, stop), base + 128, WIDE):
            kept = jnp.where((col >= stop - WIDE) & (col < stop), 0.0, t_ref[top : top + WIDE])
            t_ref[top : top + WIDE] = kept - product[top - base : top - base + WIDE]


def factor_block(w_ref, off, spare):
    full = (8, 128)
    sub = lax.broadcasted_iota(jnp.int32, full, 0)
    for j0 in range(0, WIDE, 8):
        c0 = off + j0
        rows = [w_ref[pl.ds(j0 + i, 8, stride=0), :] for i in range(8)]
        a = {}
        for i in range(8):
            for j in range(i, 8):
                a[i, j] = jnp.broadcast_to(rows[i][:, c0 + j : c0 + j + 1], full)
        left, scaled, final = {}, {}, {}
        for k in range(0, 8, 2):
            n = k + 1
            top, mid, low = a[k, k], a[k, n], a[n, n]
            rdet = 1.0 / (top * low - mid * mid)
            p = {i: low * a[k, i] - mid * a[n, i] for i in range(k + 2, 8)}
            q = {i: top * a[n, i] - mid * a[k, i] for i in range(k + 2, 8)}
            for i in range(k + 2, 8):
                for j in range(i, 8):
                    a[i, j] = a[i, j] - (p[i] * a[k, j] + q[i] * a[n, j]) * rdet
                left[k, i], left[n, i] = p[i] * rdet, q[i] * rdet
                rows[i] = rows[i] - (left[k, i] * rows[k] + left[n, i] * rows[n])
            scaled[k] = (low * rows[k] - mid * rows[n]) * rdet
            scaled[n] = (top * rows[n] - mid * rows[k]) * rdet
            root = lax.rsqrt(top)
            ratio = mid * root * root
            final[k] = rows[k] * root
            final[n] = (rows[n] - ratio * rows[k]) * lax.rsqrt(low - mid * ratio)
        for k in reversed(range(8)):
            for i in reversed(range(k // 2 * 2 + 2, 8)):
                scaled[k] = scaled[k] - left[k, i] * scaled[i]
        for q in range(j0 + 8, WIDE, 8):
            old = w_ref[q : q + 8]
            rest = old
            for k in reversed(range(8)):
                rest = rest - jnp.broadcast_to(old[:, c0 + k : c0 + k + 1], full) * scaled[k]
            w_ref[q : q + 8] = rest
        out = final[0]
        for k in range(1, 8):
            out = jnp.where(sub == k, final[k], out)
        w_ref[j0 : j0 + 8] = out
        if spare:
            spare.pop(0)()


def factor_invert(t_ref, u_ref, x_ref, w_ref, spare):
    order = t_ref.shape[0]
    lane = lax.broadcasted_iota(jnp.int32, (WIDE, 128), 1)
    sub = lax.broadcasted_iota(jnp.int32, (WIDE, 128), 0)
    for b0 in range(0, order, WIDE):
        stop = b0 + WIDE
        half, off = b0 // 128, b0 % 128
        inside = (lane >= off) & (lane < off + WIDE)
        here = slice(128 * half, 128 * half + 128)
        w_ref[:WIDE] = jnp.where(inside, t_ref[b0:stop, here], jnp.where(lane == sub + (WIDE - off), 1.0, 0.0))
        factor_block(w_ref, off, spare if b0 >= order // 2 else [])
        done = w_ref[:WIDE]
        moved = pltpu.roll(done, 64, 1)
        low, high = (moved, done) if off == 0 else (done, moved)
        x1, x2, x3 = parts_of(low)
        y1, y2, _ = parts_of(high)
        r1, r2, r3 = parts_of(t_ref[b0:stop])
        pair = lambda p, q: jnp.where(lane < WIDE, p, q)
        first = jnp.concatenate([pair(x1, y1), pair(x2, y1), pair(x3, y2)], axis=1).astype(jnp.bfloat16)
        second = jnp.concatenate([r1, r2, r1, r3, r1, r2], axis=0).astype(jnp.bfloat16)
        rows = jnp.dot(first, second, preferred_element_type=jnp.float32)
        upper, solved = [], []
        for h in range(order // 128):
            wide = rows[:, 128 * h : 128 * h + 128]
            zero = jnp.zeros_like(wide)
            if h == half:
                upper.append(jnp.where(inside, jnp.where(lane - off >= sub, done, 0.0), jnp.where(lane >= off + WIDE, wide, 0.0)))
                solved.append(jnp.where(inside, moved, jnp.where(lane < off, wide, 0.0)))
            else:
                upper.append(wide if h > half else zero)
                solved.append(wide if h < half else zero)
        upper, solved = jnp.concatenate(upper, axis=1), jnp.concatenate(solved, axis=1)
        u_ref[b0:stop] = upper
        x_ref[b0:stop] = solved
        if stop < order:
            eliminate_below(t_ref, upper, solved, stop)


def wall_diff(plane, count):
    total = jnp.zeros((count, plane.shape[1]), jnp.float32)
    for k, weight in zip((1, 2, 3), COEFS):
        total = total + weight * (plane[3 + k : 3 + k + count] - plane[3 - k : 3 - k + count])
    return total


def span_diff(band, edges):
    past, before = edges
    cells = band.shape[1]
    lane = lax.broadcasted_iota(jnp.int32, band.shape, 1)
    total = jnp.zeros(band.shape, jnp.float32)
    for k, weight in zip((1, 2, 3), COEFS):
        ahead = pltpu.roll(jnp.where(lane < k, past, band), cells - k, 1)
        behind = pltpu.roll(jnp.where(lane >= cells - k, before, band), k, 1)
        total = total + weight * (ahead - behind)
    return total


def stream_diff(planes, at):
    total = jnp.zeros(planes[0].shape, jnp.float32)
    for k, weight in zip((1, 2, 3), COEFS):
        total = total + weight * (planes[at + k] - planes[at - k])
    return total


def span_edges(rim_ref, which, turn_ref):
    snaps, slabs, _, _, rows = rim_ref.shape
    groups = [(s, i) for s in range(snaps) for i in range(slabs)]
    room = turn_ref.shape[0]
    edges = {}
    for start in range(0, len(groups), room // 8):
        some = groups[start : start + room // 8]
        turn_ref[...] = jnp.zeros_like(turn_ref)
        for g, (s, i) in enumerate(some):
            for at, entry in enumerate((3, 4, 5, None, None, 0, 1, 2)):
                if entry is not None:
                    turn_ref[8 * g + at : 8 * g + at + 1, :rows] = rim_ref[s, i, entry, which : which + 1, :]
        turned = turn_ref[...].T[:rows]
        for g, key in enumerate(some):
            edges[key] = (
                pltpu.roll(turned, (room - 8 * g) % room, 1),
                pltpu.roll(turned, (room - 8 - 8 * g) % room, 1),
            )
    return edges


def gain_matrix(omega, rows):
    snaps, rank = omega.shape
    high = omega.astype(jnp.bfloat16).astype(jnp.float32)
    low = omega - high
    pieces = [jnp.broadcast_to(part[s : s + 1], (rows, rank)) for part in (high, high, low) for s in range(snaps)]
    depth = 3 * snaps * rows
    pieces.append(jnp.zeros((-depth % 128, rank), jnp.float32))
    return jnp.concatenate(pieces, axis=0).astype(jnp.bfloat16)


def update_block(vort, right, new_ref, acc_ref):
    rows, cells, rank = new_ref.shape
    high = [v.astype(jnp.bfloat16).astype(jnp.float32) for v in vort]
    low = [v - h for v, h in zip(vort, high)]
    depth = right.shape[0]
    rest = jnp.zeros((depth - 3 * rows * len(vort), cells), jnp.float32)
    turned = jnp.concatenate(high + low + high + [rest], axis=0).T.astype(jnp.bfloat16)
    lane = lax.broadcasted_iota(jnp.int32, (1, depth), 1)
    for y in range(rows):
        mask = jnp.where(lax.rem(lane, rows) == y, 1.0, 0.0).astype(jnp.bfloat16)
        gain = jnp.dot(turned * mask, right, preferred_element_type=jnp.float32)
        new_ref[y] = (new_ref[y].astype(jnp.float32) + gain).astype(jnp.bfloat16)
    block = new_ref[...].reshape(rows * cells, rank)
    acc_ref[...] += lax.dot_general(block, block, (((0,), (0,)), ((), ())), preferred_element_type=jnp.float32)


def start_kernel(vel_in, rim_in, omega_in, band_ref, vel_ref, rim_ref, omega_ref, sems):
    snaps, _, slabs, height, _ = vel_ref.shape
    rows = height - 6
    copies = [
        pltpu.make_async_copy(source, target, sems.at[n])
        for n, (source, target) in enumerate(((vel_in, vel_ref), (rim_in, rim_ref), (omega_in, omega_ref)))
    ]
    for copy in copies:
        copy.start()
    copies[0].wait()
    for s in range(snaps):
        for c in range(2):
            for i in range(slabs):
                at = ((s * 2 + c) * slabs + i) * rows
                band_ref[at : at + rows] = vel_ref[s, 1 + c, i, 3 : 3 + rows]
    for copy in copies[1:]:
        copy.wait()


def first_component_kernel(
    vel_ref, rim_ref, omega_ref, old_ref,
    x_ref, y_ref, z_ref, gram_ref, right_ref, part_ref, turn_ref, sems,
):
    snaps, _, slabs, height, _ = vel_ref.shape
    rows = height - 6
    copies = [
        pltpu.make_async_copy(old_ref.at[c, i], new_ref.at[i], sems.at[c, i])
        for c, new_ref in enumerate((x_ref, y_ref, z_ref))
        for i in range(slabs)
    ]
    for copy in copies:
        copy.start()
    gram_ref[...] = jnp.zeros_like(gram_ref)
    right = gain_matrix(omega_ref[...], rows)
    right_ref[...] = right
    edges = span_edges(rim_ref, 0, turn_ref)
    for s in range(snaps):
        for i in range(slabs):
            part_ref[0, s, i] = span_diff(vel_ref[s, 0, i, 3 : 3 + rows], edges[s, i])
            part_ref[1, s, i] = wall_diff(vel_ref[s, 0, i], rows)
    edges = span_edges(rim_ref, 1, turn_ref)
    for i in range(slabs):
        vort = [
            wall_diff(vel_ref[s, 2, i], rows) - span_diff(vel_ref[s, 1, i, 3 : 3 + rows], edges[s, i])
            for s in range(snaps)
        ]
        copies[i].wait()
        update_block(vort, right, x_ref.at[i], gram_ref)
    for copy in copies[slabs:]:
        copy.wait()


def pack(gram_ref, first, keep_ref, send_ref):
    half = gram_ref.shape[0] // 2
    row = lax.broadcasted_iota(jnp.int32, (half, half), 0)
    col = lax.broadcasted_iota(jnp.int32, (half, half), 1)
    low = gram_ref[half:, half:]
    mixed = jnp.where(row <= col, gram_ref[:half, :half], low)
    diag = jnp.sum(jnp.where(row == col, low, 0.0), axis=0, keepdims=True)
    packed = jnp.concatenate([gram_ref[:half, half:], mixed], axis=1)
    part = half // 2
    extra = jnp.broadcast_to(jnp.concatenate([diag, diag], axis=1), (8, 2 * half))
    upper, lower = packed[:part], packed[part:]
    keep_ref[:part] = jnp.where(first, upper, lower)
    send_ref[:part] = jnp.where(first, lower, upper)
    keep_ref[part:] = extra
    send_ref[part:] = extra


def other_components_kernel(
    parity_ref, vel_ref, part_ref, inner_ref, outer_ref, right_ref, start_ref, old_y_ref, old_z_ref,
    y_ref, z_ref, keep_ref, send_ref, wide_ref, gram_ref,
):
    del old_y_ref, old_z_ref
    snaps, _, slabs, height, _ = vel_ref.shape
    rows = height - 6
    gram_ref[...] = start_ref[...]
    right = right_ref[...]
    even = parity_ref[0] == 0
    for s in range(snaps):
        for c in range(2):
            for k in range(3):
                at = ((s * 2 + c) * 3 + k) * rows
                inner, outer = inner_ref[at : at + rows], outer_ref[at : at + rows]
                wide_ref[s, c, k] = jnp.where(even, outer, inner)
                wide_ref[s, c, 3 + slabs + k] = jnp.where(even, inner, outer)
            for i in range(slabs):
                wide_ref[s, c, 3 + i] = vel_ref[s, 1 + c, i, 3 : 3 + rows]
    for i in range(slabs):
        for c, new_ref in enumerate((y_ref, z_ref)):
            vort = []
            for s in range(snaps):
                along = stream_diff([wide_ref[s, 1 - c, i + k] for k in range(7)], 3)
                if c == 0:
                    vort.append(part_ref[0, s, i] - along)
                else:
                    vort.append(along - part_ref[1, s, i])
            update_block(vort, right, new_ref.at[i], gram_ref)
    pack(gram_ref, even, keep_ref, send_ref)


def unpack(packed, part_diag, work_ref):
    half = packed.shape[0]
    cross, mixed = packed[:, :half], packed[:, half:]
    row = lax.broadcasted_iota(jnp.int32, (half, half), 0)
    col = lax.broadcasted_iota(jnp.int32, (half, half), 1)
    turned = mixed.T
    diag = jnp.broadcast_to(part_diag[:, :half], (half, half))
    work_ref[:half, :half] = jnp.where(row <= col, mixed, turned)
    work_ref[:half, half:] = cross
    work_ref[half:, :half] = cross.T
    work_ref[half:, half:] = jnp.where(row > col, mixed, jnp.where(row < col, turned, diag))


def basis_kernel(
    scale, parity_ref, mine_ref, other_ref, x_ref, y_ref, z_ref, factor_ref, basis_ref,
    work_ref, upper_ref, solved_ref, block_ref, low_ref, high_ref, factor_sem, sems,
):
    order = work_ref.shape[0]
    part = order // 4
    first = parity_ref[0] == 0
    mine, other = mine_ref[...] * scale, other_ref[...] * scale
    top, bottom = jnp.where(first, mine[:part], other[:part]), jnp.where(first, other[:part], mine[:part])
    unpack(jnp.concatenate([top, bottom], axis=0), mine[part : part + 1], work_ref)
    half = order // 2
    blocks = [(c, i, ref) for c, ref in enumerate((x_ref, y_ref, z_ref)) for i in range(ref.shape[0])]
    copies = []

    def multiply(c, i, sketch_ref, stage_ref, side, get_inverse):
        _, rows, cells, _ = sketch_ref.shape
        depth = half * (side + 1)
        step = 2 - rows % 2
        for y in range(0, rows, step):
            block = sketch_ref[i, y : y + step, :, :depth].reshape(step * cells, depth)
            product = jnp.dot(block, get_inverse(), preferred_element_type=jnp.float32)
            stage_ref[c, i, y : y + step] = product.astype(jnp.bfloat16).reshape(step, cells, half)
        columns = pl.ds(half * side, half)
        copy = pltpu.make_async_copy(
            stage_ref.at[c, i], basis_ref.at[c, i, :, :, columns], sems.at[side, c, i]
        )
        copy.start()
        copies.append(copy)

    made = []

    def first_inverse():
        if not made:
            made.append(solved_ref[:half, :half].T.astype(jnp.bfloat16))
        return made[0]

    spare = [functools.partial(multiply, *block, low_ref, 0, first_inverse) for block in blocks]
    factor_invert(work_ref, upper_ref, solved_ref, block_ref, spare)
    for piece in spare:
        piece()
    factor_copy = pltpu.make_async_copy(upper_ref, factor_ref, factor_sem)
    factor_copy.start()
    inverse = solved_ref[half:].T.astype(jnp.bfloat16)
    for block in blocks:
        multiply(*block, high_ref, 1, lambda: inverse)
    for copy in [factor_copy] + copies:
        copy.wait()


def local(velocity, span_rim, sketch_old, omega):
    snaps, _, slabs, height, cells = velocity.shape
    rows = height - 6
    rank = omega.shape[1]
    count = lax.axis_size("gx")
    limit = pltpu.CompilerParams(vmem_limit_bytes=24 << 20)
    place = lax.axis_index("gx")
    parity = (place % 2).reshape(1)
    rim = span_rim.transpose(0, 2, 4, 1, 3)
    block = (slabs, rows, cells, rank)
    square = jax.ShapeDtypeStruct((rank, rank), jnp.float32)
    held = pltpu.VMEM(block, jnp.bfloat16)
    old = pltpu.with_memory_space_constraint(sketch_old, pltpu.HBM)
    small = [pltpu.with_memory_space_constraint(x, pltpu.HBM) for x in (velocity, rim, omega)]
    planes, near_vel, near_rim, near_omega = pl.pallas_call(
        start_kernel,
        out_shape=[pltpu.VMEM((snaps * 2 * slabs * rows, cells), jnp.float32)]
        + [pltpu.VMEM(x.shape, x.dtype) for x in (velocity, rim, omega)],
        in_specs=[IN_HBM] * 3,
        out_specs=[IN_VMEM] * 4,
        scratch_shapes=[pltpu.SemaphoreType.DMA((3,))],
        compiler_params=limit,
    )(*small)
    inner, outer = planes, planes
    if slabs > 3:
        whole = planes.reshape(snaps * 2, slabs, rows, cells)
        head, tail = (x.reshape(-1, cells) for x in (whole[:, :3], whole[:, slabs - 3 :]))
        even = place % 2 == 0
        inner, outer = jnp.where(even, tail, head), jnp.where(even, head, tail)
    ring = lambda i: i % count
    outer = lax.ppermute(outer, "gx", [(i, ring(i + (1 if i % 2 else -1))) for i in range(count)])
    inner = lax.ppermute(inner, "gx", [(i, i ^ 1) for i in range(count)])
    depth = 3 * snaps * rows
    sketch_x, raw_y, raw_z, gram, right, partial = pl.pallas_call(
        first_component_kernel,
        out_shape=[held, held, held, square]
        + [pltpu.VMEM((depth + -depth % 128, rank), jnp.bfloat16)]
        + [pltpu.VMEM((2, snaps, slabs, rows, cells), jnp.float32)],
        in_specs=[IN_VMEM] * 3 + [IN_HBM],
        out_specs=[IN_VMEM] * 6,
        scratch_shapes=[pltpu.VMEM((128, 128), jnp.float32), pltpu.SemaphoreType.DMA((3, slabs))],
        compiler_params=limit,
    )(near_vel, near_rim, near_omega, old)
    piece = jax.ShapeDtypeStruct((rank // 4 + 8, rank), jnp.float32)
    sketch_y, sketch_z, keep, send = pl.pallas_call(
        other_components_kernel,
        out_shape=[held, held, piece, piece],
        in_specs=[IN_SMEM] + [IN_VMEM] * 8,
        out_specs=[IN_VMEM] * 4,
        scratch_shapes=[
            pltpu.VMEM((snaps, 2, slabs + 6, rows, cells), jnp.float32),
            pltpu.VMEM((rank, rank), jnp.float32),
        ],
        input_output_aliases={7: 0, 8: 1},
        compiler_params=limit,
    )(parity, near_vel, partial, inner, outer, right, gram, raw_y, raw_z)
    swap = lambda k: [(i, i ^ k) for i in range(count)]
    total = keep + lax.ppermute(send, "gx", swap(1))
    step = 2
    while step < count:
        total = total + lax.ppermute(total, "gx", swap(step))
        step *= 2
    other = lax.ppermute(total, "gx", swap(1))
    entries = 3 * slabs * rows * cells * count
    factor, basis = pl.pallas_call(
        functools.partial(basis_kernel, 1.0 / entries),
        out_shape=[square, jax.ShapeDtypeStruct((3, *block), jnp.bfloat16)],
        in_specs=[IN_SMEM] + [IN_VMEM] * 5,
        out_specs=[IN_HBM, IN_HBM],
        scratch_shapes=[
            pltpu.VMEM((rank, rank), jnp.float32),
            pltpu.VMEM((rank, rank), jnp.float32),
            pltpu.VMEM((rank, rank), jnp.float32),
            pltpu.VMEM((WIDE + 8, 128), jnp.float32),
            pltpu.VMEM((3, *block[:-1], rank // 2), jnp.bfloat16),
            pltpu.VMEM((3, *block[:-1], rank // 2), jnp.bfloat16),
            pltpu.SemaphoreType.DMA,
            pltpu.SemaphoreType.DMA((2, 3, slabs)),
        ],
        compiler_params=limit,
    )(parity, total, other, sketch_x, sketch_y, sketch_z)
    return basis, factor


def solution(mesh):
    in_specs = (
        P(None, None, ("rec", "gx"), None, None),
        P(None, None, ("rec", "gx"), None, None),
        P(None, ("rec", "gx"), None, None, None),
        P(),
    )
    out_specs = (P(None, ("rec", "gx"), None, None, None), P("rec", None))
    return jax.shard_map(local, mesh=mesh, in_specs=in_specs, out_specs=out_specs, check_vma=False)
```

```python
import functools

import jax
import jax.numpy as jnp
from jax import lax
from jax.experimental import pallas as pl
from jax.experimental.pallas import tpu as pltpu
from jax.sharding import PartitionSpec as P

COEFS = (0.75, -0.15, 1.0 / 60.0)
IN_SMEM = pl.BlockSpec(memory_space=pltpu.SMEM)
IN_VMEM = pl.BlockSpec(memory_space=pltpu.VMEM)
IN_HBM = pl.BlockSpec(memory_space=pltpu.HBM)
WIDE = 64


def parts_of(x):
    high = x.astype(jnp.bfloat16).astype(jnp.float32)
    rest = x - high
    mid = rest.astype(jnp.bfloat16).astype(jnp.float32)
    return high, mid, rest - mid


def eliminate_below(t_ref, upper, solved, stop):
    order = t_ref.shape[0]
    col = lax.broadcasted_iota(jnp.int32, upper.shape, 1)
    v, w, y = parts_of(jnp.where(col < stop, solved, upper))
    right = jnp.concatenate([v, w, v, y, v, w], axis=0).astype(jnp.bfloat16)
    for base in range(stop // 128 * 128, order, 128):
        a, b, c = parts_of(upper[:, base : base + 128])
        left = jnp.concatenate([a, a, b, a, c, b], axis=0).astype(jnp.bfloat16)
        product = lax.dot_general(left, right, (((0,), (0,)), ((), ())), preferred_element_type=jnp.float32)
        for top in range(max(base, stop), base + 128, WIDE):
            kept = jnp.where((col >= stop - WIDE) & (col < stop), 0.0, t_ref[top : top + WIDE])
            t_ref[top : top + WIDE] = kept - product[top - base : top - base + WIDE]


def factor_block(w_ref, off, spare):
    full = (8, 128)
    sub = lax.broadcasted_iota(jnp.int32, full, 0)
    for j0 in range(0, WIDE, 8):
        c0 = off + j0
        rows = [w_ref[pl.ds(j0 + i, 8, stride=0), :] for i in range(8)]
        a = {}
        for i in range(8):
            for j in range(i, 8):
                a[i, j] = jnp.broadcast_to(rows[i][:, c0 + j : c0 + j + 1], full)
        left, scaled, final = {}, {}, {}
        for k in range(0, 8, 2):
            n = k + 1
            top, mid, low = a[k, k], a[k, n], a[n, n]
            rdet = 1.0 / (top * low - mid * mid)
            p = {i: low * a[k, i] - mid * a[n, i] for i in range(k + 2, 8)}
            q = {i: top * a[n, i] - mid * a[k, i] for i in range(k + 2, 8)}
            for i in range(k + 2, 8):
                for j in range(i, 8):
                    a[i, j] = a[i, j] - (p[i] * a[k, j] + q[i] * a[n, j]) * rdet
                left[k, i], left[n, i] = p[i] * rdet, q[i] * rdet
                rows[i] = rows[i] - (left[k, i] * rows[k] + left[n, i] * rows[n])
            scaled[k] = (low * rows[k] - mid * rows[n]) * rdet
            scaled[n] = (top * rows[n] - mid * rows[k]) * rdet
            root = lax.rsqrt(top)
            ratio = mid * root * root
            final[k] = rows[k] * root
            final[n] = (rows[n] - ratio * rows[k]) * lax.rsqrt(low - mid * ratio)
        for k in reversed(range(8)):
            for i in reversed(range(k // 2 * 2 + 2, 8)):
                scaled[k] = scaled[k] - left[k, i] * scaled[i]
        for q in range(j0 + 8, WIDE, 8):
            old = w_ref[q : q + 8]
            rest = old
            for k in reversed(range(8)):
                rest = rest - jnp.broadcast_to(old[:, c0 + k : c0 + k + 1], full) * scaled[k]
            w_ref[q : q + 8] = rest
        out = final[0]
        for k in range(1, 8):
            out = jnp.where(sub == k, final[k], out)
        w_ref[j0 : j0 + 8] = out
        if spare:
            spare.pop(0)()


def factor_invert(t_ref, u_ref, x_ref, w_ref, spare):
    order = t_ref.shape[0]
    lane = lax.broadcasted_iota(jnp.int32, (WIDE, 128), 1)
    sub = lax.broadcasted_iota(jnp.int32, (WIDE, 128), 0)
    for b0 in range(0, order, WIDE):
        stop = b0 + WIDE
        half, off = b0 // 128, b0 % 128
        inside = (lane >= off) & (lane < off + WIDE)
        here = slice(128 * half, 128 * half + 128)
        w_ref[:WIDE] = jnp.where(inside, t_ref[b0:stop, here], jnp.where(lane == sub + (WIDE - off), 1.0, 0.0))
        factor_block(w_ref, off, spare if b0 >= order // 2 else [])
        done = w_ref[:WIDE]
        moved = pltpu.roll(done, 64, 1)
        low, high = (moved, done) if off == 0 else (done, moved)
        x1, x2, x3 = parts_of(low)
        y1, y2, _ = parts_of(high)
        r1, r2, r3 = parts_of(t_ref[b0:stop])
        pair = lambda p, q: jnp.where(lane < WIDE, p, q)
        first = jnp.concatenate([pair(x1, y1), pair(x2, y1), pair(x3, y2)], axis=1).astype(jnp.bfloat16)
        second = jnp.concatenate([r1, r2, r1, r3, r1, r2], axis=0).astype(jnp.bfloat16)
        rows = jnp.dot(first, second, preferred_element_type=jnp.float32)
        upper, solved = [], []
        for h in range(order // 128):
            wide = rows[:, 128 * h : 128 * h + 128]
            zero = jnp.zeros_like(wide)
            if h == half:
                upper.append(jnp.where(inside, jnp.where(lane - off >= sub, done, 0.0), jnp.where(lane >= off + WIDE, wide, 0.0)))
                solved.append(jnp.where(inside, moved, jnp.where(lane < off, wide, 0.0)))
            else:
                upper.append(wide if h > half else zero)
                solved.append(wide if h < half else zero)
        upper, solved = jnp.concatenate(upper, axis=1), jnp.concatenate(solved, axis=1)
        u_ref[b0:stop] = upper
        x_ref[b0:stop] = solved
        if stop < order:
            eliminate_below(t_ref, upper, solved, stop)


def wall_diff(plane, count):
    total = jnp.zeros((count, plane.shape[1]), jnp.float32)
    for k, weight in zip((1, 2, 3), COEFS):
        total = total + weight * (plane[3 + k : 3 + k + count] - plane[3 - k : 3 - k + count])
    return total


def span_diff(band, edges):
    past, before = edges
    cells = band.shape[1]
    lane = lax.broadcasted_iota(jnp.int32, band.shape, 1)
    total = jnp.zeros(band.shape, jnp.float32)
    for k, weight in zip((1, 2, 3), COEFS):
        ahead = pltpu.roll(jnp.where(lane < k, past, band), cells - k, 1)
        behind = pltpu.roll(jnp.where(lane >= cells - k, before, band), k, 1)
        total = total + weight * (ahead - behind)
    return total


def stream_diff(planes, at):
    total = jnp.zeros(planes[0].shape, jnp.float32)
    for k, weight in zip((1, 2, 3), COEFS):
        total = total + weight * (planes[at + k] - planes[at - k])
    return total


def span_edges(rim_ref, which, turn_ref):
    snaps, slabs, _, _, rows = rim_ref.shape
    groups = [(s, i) for s in range(snaps) for i in range(slabs)]
    room = turn_ref.shape[0]
    edges = {}
    for start in range(0, len(groups), room // 8):
        some = groups[start : start + room // 8]
        turn_ref[...] = jnp.zeros_like(turn_ref)
        for g, (s, i) in enumerate(some):
            for at, entry in enumerate((3, 4, 5, None, None, 0, 1, 2)):
                if entry is not None:
                    turn_ref[8 * g + at : 8 * g + at + 1, :rows] = rim_ref[s, i, entry, which : which + 1, :]
        turned = turn_ref[...].T[:rows]
        for g, key in enumerate(some):
            edges[key] = (
                pltpu.roll(turned, (room - 8 * g) % room, 1),
                pltpu.roll(turned, (room - 8 - 8 * g) % room, 1),
            )
    return edges


def gain_matrix(omega, rows):
    snaps, rank = omega.shape
    high = omega.astype(jnp.bfloat16).astype(jnp.float32)
    low = omega - high
    pieces = [jnp.broadcast_to(part[s : s + 1], (rows, rank)) for part in (high, high, low) for s in range(snaps)]
    depth = 3 * snaps * rows
    pieces.append(jnp.zeros((-depth % 128, rank), jnp.float32))
    return jnp.concatenate(pieces, axis=0).astype(jnp.bfloat16)


def update_block(vort, right, new_ref, acc_ref):
    rows, cells, rank = new_ref.shape
    high = [v.astype(jnp.bfloat16).astype(jnp.float32) for v in vort]
    low = [v - h for v, h in zip(vort, high)]
    depth = right.shape[0]
    rest = jnp.zeros((depth - 3 * rows * len(vort), cells), jnp.float32)
    turned = jnp.concatenate(high + low + high + [rest], axis=0).T.astype(jnp.bfloat16)
    lane = lax.broadcasted_iota(jnp.int32, (1, depth), 1)
    for y in range(rows):
        mask = jnp.where(lax.rem(lane, rows) == y, 1.0, 0.0).astype(jnp.bfloat16)
        gain = jnp.dot(turned * mask, right, preferred_element_type=jnp.float32)
        new_ref[y] = (new_ref[y].astype(jnp.float32) + gain).astype(jnp.bfloat16)
    block = new_ref[...].reshape(rows * cells, rank)
    acc_ref[...] += lax.dot_general(block, block, (((0,), (0,)), ((), ())), preferred_element_type=jnp.float32)


def start_kernel(vel_in, rim_in, omega_in, v_ref, w_ref, vel_ref, rim_ref, omega_ref, sems):
    snaps, _, slabs, height, _ = vel_ref.shape
    rows = height - 6
    copies = [
        pltpu.make_async_copy(source, target, sems.at[n])
        for n, (source, target) in enumerate(((vel_in, vel_ref), (rim_in, rim_ref), (omega_in, omega_ref)))
    ]
    for copy in copies:
        copy.start()
    copies[0].wait()
    for s in range(snaps):
        for c in range(2):
            for i in range(slabs):
                at = (s * slabs + i) * rows
                (v_ref, w_ref)[c][at : at + rows] = vel_ref[s, 1 + c, i, 3 : 3 + rows]
    for copy in copies[1:]:
        copy.wait()


def first_component_kernel(
    vel_ref, rim_ref, omega_ref, old_ref,
    x_ref, y_ref, z_ref, gram_ref, right_ref, part_ref, turn_ref, sems,
):
    snaps, _, slabs, height, _ = vel_ref.shape
    rows = height - 6
    copies = [
        pltpu.make_async_copy(old_ref.at[c, i], new_ref.at[i], sems.at[c, i])
        for c, new_ref in enumerate((x_ref, y_ref, z_ref))
        for i in range(slabs)
    ]
    for copy in copies:
        copy.start()
    gram_ref[...] = jnp.zeros_like(gram_ref)
    right = gain_matrix(omega_ref[...], rows)
    right_ref[...] = right
    edges = span_edges(rim_ref, 0, turn_ref)
    for s in range(snaps):
        for i in range(slabs):
            part_ref[0, s, i] = span_diff(vel_ref[s, 0, i, 3 : 3 + rows], edges[s, i])
            part_ref[1, s, i] = wall_diff(vel_ref[s, 0, i], rows)
    edges = span_edges(rim_ref, 1, turn_ref)
    for i in range(slabs):
        vort = [
            wall_diff(vel_ref[s, 2, i], rows) - span_diff(vel_ref[s, 1, i, 3 : 3 + rows], edges[s, i])
            for s in range(snaps)
        ]
        copies[i].wait()
        update_block(vort, right, x_ref.at[i], gram_ref)
    for copy in copies[slabs:]:
        copy.wait()


def pack(gram_ref, first, keep_ref, send_ref):
    half = gram_ref.shape[0] // 2
    row = lax.broadcasted_iota(jnp.int32, (half, half), 0)
    col = lax.broadcasted_iota(jnp.int32, (half, half), 1)
    low = gram_ref[half:, half:]
    mixed = jnp.where(row <= col, gram_ref[:half, :half], low)
    diag = jnp.sum(jnp.where(row == col, low, 0.0), axis=0, keepdims=True)
    packed = jnp.concatenate([gram_ref[:half, half:], mixed], axis=1)
    part = half // 2
    extra = jnp.broadcast_to(jnp.concatenate([diag, diag], axis=1), (8, 2 * half))
    upper, lower = packed[:part], packed[part:]
    keep_ref[:part] = jnp.where(first, upper, lower)
    send_ref[:part] = jnp.where(first, lower, upper)
    keep_ref[part:] = extra
    send_ref[part:] = extra


def other_component_kernel(
    which, parity_ref, vel_ref, part_ref, inner_ref, outer_ref, right_ref, start_ref, old_ref, new_ref, *rest
):
    del old_ref
    snaps, _, slabs, height, _ = vel_ref.shape
    rows = height - 6
    *outs, wide_ref, gram_ref = rest
    gram_ref[...] = start_ref[...]
    right = right_ref[...]
    even = parity_ref[0] == 0
    for s in range(snaps):
        for k in range(3):
            at = (s * 3 + k) * rows
            inner, outer = inner_ref[at : at + rows], outer_ref[at : at + rows]
            wide_ref[s, k] = jnp.where(even, outer, inner)
            wide_ref[s, 3 + slabs + k] = jnp.where(even, inner, outer)
        for i in range(slabs):
            wide_ref[s, 3 + i] = vel_ref[s, 3 - which, i, 3 : 3 + rows]
    for i in range(slabs):
        vort = []
        for s in range(snaps):
            along = stream_diff([wide_ref[s, i + k] for k in range(7)], 3)
            part = part_ref[which - 1, s, i]
            vort.append(part - along if which == 1 else along - part)
        update_block(vort, right, new_ref.at[i], gram_ref)
    if which == 1:
        outs[0][...] = gram_ref[...]
    else:
        pack(gram_ref, even, *outs)


def unpack(packed, part_diag, work_ref):
    half = packed.shape[0]
    cross, mixed = packed[:, :half], packed[:, half:]
    row = lax.broadcasted_iota(jnp.int32, (half, half), 0)
    col = lax.broadcasted_iota(jnp.int32, (half, half), 1)
    turned = mixed.T
    diag = jnp.broadcast_to(part_diag[:, :half], (half, half))
    work_ref[:half, :half] = jnp.where(row <= col, mixed, turned)
    work_ref[:half, half:] = cross
    work_ref[half:, :half] = cross.T
    work_ref[half:, half:] = jnp.where(row > col, mixed, jnp.where(row < col, turned, diag))


def basis_kernel(
    scale, parity_ref, mine_ref, other_ref, x_ref, y_ref, z_ref, factor_ref, basis_ref,
    work_ref, upper_ref, solved_ref, block_ref, low_ref, high_ref, factor_sem, sems,
):
    order = work_ref.shape[0]
    part = order // 4
    first = parity_ref[0] == 0
    mine, other = mine_ref[...] * scale, other_ref[...] * scale
    top, bottom = jnp.where(first, mine[:part], other[:part]), jnp.where(first, other[:part], mine[:part])
    unpack(jnp.concatenate([top, bottom], axis=0), mine[part : part + 1], work_ref)
    half = order // 2
    blocks = [(c, i, ref) for c, ref in enumerate((x_ref, y_ref, z_ref)) for i in range(ref.shape[0])]
    copies = []

    def multiply(c, i, sketch_ref, stage_ref, side, get_inverse):
        _, rows, cells, _ = sketch_ref.shape
        depth = half * (side + 1)
        step = 2 - rows % 2
        for y in range(0, rows, step):
            block = sketch_ref[i, y : y + step, :, :depth].reshape(step * cells, depth)
            product = jnp.dot(block, get_inverse(), preferred_element_type=jnp.float32)
            stage_ref[c, i, y : y + step] = product.astype(jnp.bfloat16).reshape(step, cells, half)
        columns = pl.ds(half * side, half)
        copy = pltpu.make_async_copy(
            stage_ref.at[c, i], basis_ref.at[c, i, :, :, columns], sems.at[side, c, i]
        )
        copy.start()
        copies.append(copy)

    made = []

    def first_inverse():
        if not made:
            made.append(solved_ref[:half, :half].T.astype(jnp.bfloat16))
        return made[0]

    spare = [functools.partial(multiply, *block, low_ref, 0, first_inverse) for block in blocks]
    factor_invert(work_ref, upper_ref, solved_ref, block_ref, spare)
    for piece in spare:
        piece()
    factor_copy = pltpu.make_async_copy(upper_ref, factor_ref, factor_sem)
    factor_copy.start()
    inverse = solved_ref[half:].T.astype(jnp.bfloat16)
    for block in blocks:
        multiply(*block, high_ref, 1, lambda: inverse)
    for copy in [factor_copy] + copies:
        copy.wait()


def local(velocity, span_rim, sketch_old, omega):
    snaps, _, slabs, height, cells = velocity.shape
    rows = height - 6
    rank = omega.shape[1]
    count = lax.axis_size("gx")
    limit = pltpu.CompilerParams(vmem_limit_bytes=24 << 20)
    place = lax.axis_index("gx")
    parity = (place % 2).reshape(1)
    rim = span_rim.transpose(0, 2, 4, 1, 3)
    block = (slabs, rows, cells, rank)
    square = jax.ShapeDtypeStruct((rank, rank), jnp.float32)
    held = pltpu.VMEM(block, jnp.bfloat16)
    old = pltpu.with_memory_space_constraint(sketch_old, pltpu.HBM)
    small = [pltpu.with_memory_space_constraint(x, pltpu.HBM) for x in (velocity, rim, omega)]
    planes_v, planes_w, near_vel, near_rim, near_omega = pl.pallas_call(
        start_kernel,
        out_shape=[pltpu.VMEM((snaps * slabs * rows, cells), jnp.float32)] * 2
        + [pltpu.VMEM(x.shape, x.dtype) for x in (velocity, rim, omega)],
        in_specs=[IN_HBM] * 3,
        out_specs=[IN_VMEM] * 5,
        scratch_shapes=[pltpu.SemaphoreType.DMA((3,))],
        compiler_params=limit,
    )(*small)
    ring = lambda i: i % count
    across = [(i, ring(i + (1 if i % 2 else -1))) for i in range(count)]
    within = [(i, i ^ 1) for i in range(count)]

    def sides(planes):
        if slabs == 3:
            return planes, planes
        whole = planes.reshape(snaps, slabs, rows, cells)
        head, tail = (x.reshape(-1, cells) for x in (whole[:, :3], whole[:, slabs - 3 :]))
        even = place % 2 == 0
        return jnp.where(even, tail, head), jnp.where(even, head, tail)

    (inner_w, outer_w), (inner_v, outer_v) = sides(planes_w), sides(planes_v)
    outer_w = lax.ppermute(outer_w, "gx", across)
    outer_v = lax.ppermute(outer_v, "gx", across)
    inner_w = lax.ppermute(inner_w, "gx", within)
    inner_v = lax.ppermute(inner_v, "gx", within)
    depth = 3 * snaps * rows
    sketch_x, raw_y, raw_z, gram, right, partial = pl.pallas_call(
        first_component_kernel,
        out_shape=[held, held, held, square]
        + [pltpu.VMEM((depth + -depth % 128, rank), jnp.bfloat16)]
        + [pltpu.VMEM((2, snaps, slabs, rows, cells), jnp.float32)],
        in_specs=[IN_VMEM] * 3 + [IN_HBM],
        out_specs=[IN_VMEM] * 6,
        scratch_shapes=[pltpu.VMEM((128, 128), jnp.float32), pltpu.SemaphoreType.DMA((3, slabs))],
        compiler_params=limit,
    )(near_vel, near_rim, near_omega, old)
    piece = jax.ShapeDtypeStruct((rank // 4 + 8, rank), jnp.float32)

    def other_component(which, outs, inner, outer, gram, raw):
        return pl.pallas_call(
            functools.partial(other_component_kernel, which),
            out_shape=[held] + outs,
            in_specs=[IN_SMEM] + [IN_VMEM] * 7,
            out_specs=[IN_VMEM] * (1 + len(outs)),
            scratch_shapes=[
                pltpu.VMEM((snaps, slabs + 6, rows, cells), jnp.float32),
                pltpu.VMEM((rank, rank), jnp.float32),
            ],
            input_output_aliases={7: 0},
            compiler_params=limit,
        )(parity, near_vel, partial, inner, outer, right, gram, raw)

    sketch_y, gram = other_component(1, [square], inner_w, outer_w, gram, raw_y)
    sketch_z, keep, send = other_component(2, [piece, piece], inner_v, outer_v, gram, raw_z)
    swap = lambda k: [(i, i ^ k) for i in range(count)]
    total = keep + lax.ppermute(send, "gx", swap(1))
    step = 2
    while step < count:
        total = total + lax.ppermute(total, "gx", swap(step))
        step *= 2
    other = lax.ppermute(total, "gx", swap(1))
    entries = 3 * slabs * rows * cells * count
    factor, basis = pl.pallas_call(
        functools.partial(basis_kernel, 1.0 / entries),
        out_shape=[square, jax.ShapeDtypeStruct((3, *block), jnp.bfloat16)],
        in_specs=[IN_SMEM] + [IN_VMEM] * 5,
        out_specs=[IN_HBM, IN_HBM],
        scratch_shapes=[
            pltpu.VMEM((rank, rank), jnp.float32),
            pltpu.VMEM((rank, rank), jnp.float32),
            pltpu.VMEM((rank, rank), jnp.float32),
            pltpu.VMEM((WIDE + 8, 128), jnp.float32),
            pltpu.VMEM((3, *block[:-1], rank // 2), jnp.bfloat16),
            pltpu.VMEM((3, *block[:-1], rank // 2), jnp.bfloat16),
            pltpu.SemaphoreType.DMA,
            pltpu.SemaphoreType.DMA((2, 3, slabs)),
        ],
        compiler_params=limit,
    )(parity, total, other, sketch_x, sketch_y, sketch_z)
    return basis, factor


def solution(mesh):
    in_specs = (
        P(None, None, ("rec", "gx"), None, None),
        P(None, None, ("rec", "gx"), None, None),
        P(None, ("rec", "gx"), None, None, None),
        P(),
    )
    out_specs = (P(None, ("rec", "gx"), None, None, None), P("rec", None))
    return jax.shard_map(local, mesh=mesh, in_specs=in_specs, out_specs=out_specs, check_vma=False)
```
